128 devices in a mesh: dp: 16 (over z, x), tm: 8 (over y, core).
Axes of the slice: x: 4, y: 4, z: 4, core: 2. Of those that a mesh axis runs over, the one named last changes fastest.
Arguments:
- frames: bfloat16 [16, 6144, 1024], P('dp', 'tm'), may hold values from -18 to 18
- lengths: int32 [16], P('dp'), may hold values from 1 to 6144, 58982 in all
- w_in: bfloat16 [1024, 2048], replicated, may hold values from -4 to 4
- w_dw: float32 [31, 1024], replicated, may hold values from -1 to 1
- bn_gain: float32 [1024], replicated, may hold values from 0.25 to 1.75
- bn_bias: float32 [1024], replicated, may hold values from -1 to 1
- w_out: bfloat16 [1024, 1024], replicated, may hold values from -0.1875 to 0.1875
- cotangent: bfloat16 [16, 6144, 1024], P('dp', 'tm'), may hold values from -6 to 6
Outputs:
- output: bfloat16 [16, 6144, 1024], P('dp', 'tm')
- grad_frames: bfloat16 [16, 6144, 1024], P('dp', 'tm')
- grad_w_in: float32 [1024, 2048], P(('dp', 'tm'))
- grad_w_out: float32 [1024, 1024], P(('dp', 'tm'))
- grad_kernel: float32 [31, 1024], replicated
- grad_gain: float32 [1024], replicated
- grad_bias: float32 [1024], replicated
The draws below stay inside these ranges and needn't reach their ends.
Inputs may be any that keep to these rules, and one draw needn't show every extreme that they name: Frame slots at or after a recording's length are padding; the lengths sum to 58982 and the longest is exactly 6144.
All inputs are finite; a program needn't handle non-finite values. No bound on the sum of `lengths` on one device may be relied on, other than what follows from the above.
Results may differ from the reference program's by a relative error of at most 0.015.
Values may be sent and summed in bfloat16 or wider, within the bound.
A program may use at most 128 MiB of HBM per device.

```python
import math
import jax
import jax.numpy as jnp
import numpy as np
from jax import lax

C = 1024
K = 31
HALO = 15
RECS = 16
LEN = 6144


def draw_frames(key, part):
    base_key, frame_key, record_key = jax.random.split(jax.random.fold_in(key, 17), 3)
    values = jax.random.truncated_normal(base_key, -4.0, 4.0, (RECS, LEN, C), jnp.float32)
    frame_scale = jnp.exp(jax.random.uniform(frame_key, (RECS, LEN, 1), jnp.float32, math.log(0.3), math.log(3.0)))
    record_scale = jnp.exp(jax.random.uniform(record_key, (RECS, 1, 1), jnp.float32, math.log(0.5), math.log(1.5)))
    return (values * frame_scale * record_scale).astype(jnp.bfloat16)


def draw_w_in(key, part):
    base_key, column_key = jax.random.split(jax.random.fold_in(key, 29), 2)
    values = jax.random.truncated_normal(base_key, -4.0, 4.0, (C, 2 * C), jnp.float32)
    column_scale = jnp.exp(jax.random.uniform(column_key, (1, 2 * C), jnp.float32, -1.15, 1.15))
    return (values * column_scale / math.sqrt(C)).astype(jnp.bfloat16)


def levels(own_key, extent, pieces, smallest, largest):
    factor_of = 1.0
    for position, parts in pieces:
        steps = jax.random.uniform(jax.random.fold_in(jax.random.fold_in(own_key, 6), position), (parts,), jnp.float32, smallest / len(pieces), largest / len(pieces))
        factor_of = factor_of * jnp.repeat(jnp.exp(steps), extent[position] // parts).reshape((-1,) + (1,) * (len(extent) - 1 - position))
    return factor_of


def profile(count, total, most, slope):
    loads = [(1 << 20) // math.isqrt(standing ** slope) + 1 for standing in range(2, count + 1)]
    rest, counts = total - most - (count - 1), [1] * (count - 1)
    while rest > 0:
        movable = [i for i in range(count - 1) if counts[i] < most]
        mass, budget = sum([loads[i] for i in movable]), rest
        for i in movable:
            addition = min(most - counts[i], max(1, budget * loads[i] // mass), rest)
            counts[i] = counts[i] + addition
            rest = rest - addition
    return np.array([most] + counts)


def uneven_parts(key, amount, total, most, lean):
    if amount == 2:
        one = jax.random.randint(key, (), max(1, total - most), min(most, total - 1) + 1)
        return jnp.stack([one, total - one])
    sizes = jnp.asarray(profile(amount, total, most, lean), jnp.int32)
    twos = (amount - 1) // 2
    giver, sink = sizes[1:1 + 2 * twos:2], sizes[2:2 + 2 * twos:2]
    slack = jnp.minimum(giver - 1, most - sink)
    moved = jax.random.randint(jax.random.fold_in(key, 1), (twos,), 0, 1 << 20) % (slack + 1)
    sizes = sizes.at[1:1 + 2 * twos:2].set(giver - moved).at[2:2 + 2 * twos:2].set(sink + moved)
    return sizes[jax.random.permutation(jax.random.fold_in(key, 2), amount)]


def normal_values(own_key, extent, scale, reach, cuts=(), kind=jnp.bfloat16):
    loudness = levels(own_key, extent, cuts, -0.22, 0.18) if cuts else 1.0
    values = jax.random.normal(own_key, extent, jnp.float32) * scale * loudness
    return jnp.minimum(jnp.maximum(values, -reach), reach).astype(kind)


def setup_inputs(seed: int = 0) -> dict:
    seeds = jax.random.split(jax.random.key(seed), 9)
    frames = draw_frames(jax.random.fold_in(seeds[8], 71), 0)
    lengths = uneven_parts(seeds[1], RECS, 3 * RECS * LEN // 5, LEN, 1).astype(jnp.int32)
    w_in = draw_w_in(jax.random.fold_in(seeds[8], 71), 0)
    w_dw = normal_values(seeds[3], (K, C), K ** -0.5, 1.0, (), jnp.float32)
    bn_gain = jnp.clip(1.0 + 0.15 * jax.random.normal(seeds[4], (C,), jnp.float32), 0.25, 1.75)
    bn_bias = jnp.clip(jax.random.uniform(seeds[5], (C,), jnp.float32, -1.0, 1.0), -1.0, 1.0)
    w_out = normal_values(seeds[6], (C, C), C ** -0.5, 0.1875)
    cotangent = normal_values(seeds[7], (RECS, LEN, C), 1.0, 6.0, ((0, 16), (1, 8)))
    return {"frames": frames, "lengths": lengths, "w_in": w_in, "w_dw": w_dw, "bn_gain": bn_gain, "bn_bias": bn_bias, "w_out": w_out, "cotangent": cotangent}


def taps_forward(padded, kernel, frame_count):
    summed = jnp.zeros((frame_count, padded.shape[1]), jnp.float32)
    for tap_index in range(kernel.shape[0]):
        summed = summed + kernel[tap_index] * padded[tap_index:tap_index + frame_count].astype(jnp.float32)
    return summed

def taps_backward(padded_grad, kernel, frame_count):
    reach_both = kernel.shape[0] - 1
    summed = jnp.zeros((frame_count, padded_grad.shape[1]), jnp.float32)
    for tap_index in range(kernel.shape[0]):
        begin = reach_both - tap_index
        summed = summed + kernel[tap_index] * padded_grad[begin:begin + frame_count].astype(jnp.float32)
    return summed

def taps_kernel(padded_glu, dconv_rows, kernel_taps, frame_count):
    grad_rows = dconv_rows.astype(jnp.float32)
    tap_rows = []
    for tap_index in range(kernel_taps):
        tap_rows.append(lax.optimization_barrier(jnp.sum(padded_glu[tap_index:tap_index + frame_count].astype(jnp.float32) * grad_rows, axis=0)))
    return jnp.stack(tap_rows)

def front(rec_frames, rec_length, w_in, w_dw):
    live_rows = (jnp.arange(LEN, dtype=jnp.int32) < rec_length).astype(jnp.float32)[:, None]
    pre_act = jnp.dot(rec_frames, w_in, preferred_element_type=jnp.float32)
    linear_half = pre_act[:, :C]
    gate_sig = jax.nn.sigmoid(pre_act[:, C:])
    glu_out = (linear_half * gate_sig * live_rows).astype(jnp.bfloat16)
    padded = jnp.pad(glu_out, ((HALO, HALO), (0, 0)))
    conv_out = taps_forward(padded, w_dw, LEN)
    return (live_rows, linear_half, gate_sig, padded, conv_out)

def middle(conv_out, live_rows, mean_vec, inv_std, bn_gain, bn_bias):
    normed = (conv_out - mean_vec) * inv_std
    shifted = bn_gain * normed + bn_bias
    act_sig = jax.nn.sigmoid(shifted)
    swished = (shifted * act_sig * live_rows).astype(jnp.bfloat16)
    return (normed, shifted, act_sig, swished)

def shift_grad(rec_cot, w_out, live_rows, shifted, act_sig):
    dswish = jnp.dot(rec_cot, w_out.T, preferred_element_type=jnp.float32)
    return live_rows * dswish * act_sig * (1.0 + shifted * (1.0 - act_sig))

def reference(frames, lengths, w_in, w_dw, bn_gain, bn_bias, w_out, cotangent):

    def moments(item):
        rec_frames, rec_length = item
        live_rows, linear_half, gate_sig, padded, conv_out = front(rec_frames, rec_length, w_in, w_dw)
        return (lax.optimization_barrier(jnp.sum(conv_out * live_rows, axis=0)), lax.optimization_barrier(jnp.sum(conv_out * conv_out * live_rows, axis=0)))
    sums_all, squares_all = lax.map(moments, (frames, lengths))
    count = jnp.sum(lengths).astype(jnp.float32)
    mean_vec = lax.optimization_barrier(jnp.sum(sums_all, axis=0)) / count
    variance = lax.optimization_barrier(jnp.sum(squares_all, axis=0)) / count - mean_vec * mean_vec
    inv_std = lax.rsqrt(variance + 1e-05)

    def second(item):
        rec_frames, rec_length, rec_cot = item
        live_rows, linear_half, gate_sig, padded, conv_out = front(rec_frames, rec_length, w_in, w_dw)
        normed, shifted, act_sig, swished = middle(conv_out, live_rows, mean_vec, inv_std, bn_gain, bn_bias)
        out_rows = jnp.dot(swished, w_out, preferred_element_type=jnp.float32).astype(jnp.bfloat16)
        dshift = shift_grad(rec_cot, w_out, live_rows, shifted, act_sig)
        return (out_rows, lax.optimization_barrier(jnp.sum(dshift * normed, axis=0)), lax.optimization_barrier(jnp.sum(dshift, axis=0)))
    output, gain_parts, bias_parts = lax.map(second, (frames, lengths, cotangent))
    sum_gain = lax.optimization_barrier(jnp.sum(gain_parts, axis=0))
    sum_bias = lax.optimization_barrier(jnp.sum(bias_parts, axis=0))

    def third(carry_pair, item):
        weight_sum, kernel_sum = carry_pair
        rec_frames, rec_length, rec_cot = item
        live_rows, linear_half, gate_sig, padded, conv_out = front(rec_frames, rec_length, w_in, w_dw)
        normed, shifted, act_sig, swished = middle(conv_out, live_rows, mean_vec, inv_std, bn_gain, bn_bias)
        dshift = shift_grad(rec_cot, w_out, live_rows, shifted, act_sig)
        dconv = (live_rows * bn_gain * inv_std * (dshift - sum_bias / count - normed * sum_gain / count)).astype(jnp.bfloat16)
        padded_grad = jnp.pad(dconv, ((HALO, HALO), (0, 0)))
        dglu = live_rows * taps_backward(padded_grad, w_dw, LEN)
        dpre = jnp.concatenate([dglu * gate_sig, dglu * linear_half * gate_sig * (1.0 - gate_sig)], axis=1).astype(jnp.bfloat16)
        grad_rows = jnp.dot(dpre, w_in.T, preferred_element_type=jnp.float32).astype(jnp.bfloat16)
        term_in = jnp.dot(rec_frames.T, dpre, preferred_element_type=jnp.float32)
        term_out = jnp.dot(swished.T, rec_cot, preferred_element_type=jnp.float32)
        weight_sum = weight_sum + jnp.concatenate([term_in, term_out], axis=1)
        kernel_sum = kernel_sum + taps_kernel(padded, dconv, K, LEN)
        return ((weight_sum, kernel_sum), grad_rows)
    start_pair = (jnp.zeros((C, 3 * C), jnp.float32), jnp.zeros((K, C), jnp.float32))
    final_pair, grad_frames = lax.scan(third, start_pair, (frames, lengths, cotangent))
    scale = 1.0 / math.sqrt(RECS * LEN)
    weight_sum, kernel_sum = final_pair
    grad_w_in = weight_sum[:, :2 * C] * scale
    grad_w_out = weight_sum[:, 2 * C:] * scale
    return (output, grad_frames, grad_w_in, grad_w_out, kernel_sum * scale, sum_gain * scale, sum_bias * scale)
```

```python
import math

import jax
import jax.numpy as jnp
from jax import lax
from jax.experimental import pallas as pl
from jax.experimental.pallas import tpu as pltpu
from jax.sharding import PartitionSpec as P

MESH_ID = pl.DeviceIdType.MESH
F32 = jnp.float32
BF16 = jnp.bfloat16

ROWS = 768
CH = 1024
CB = 8
PAD = 16
PROWS = ROWS + 2 * PAD
TAPS = 31
COUNT = 58982.0
NDP, NTM = 16, 8
GRP = 8
GROUPS = ROWS // (8 * GRP)
MB = 256
NB = 6
ORDERS = (("z", "x", "y"), ("x", "y", "z"), ("y", "z", "x"))


def sigmoid(x):
    return 0.5 * jnp.tanh(0.5 * x) + 0.5


def dot_nn(a, b):
    return lax.dot_general(a, b, (((1,), (0,)), ((), ())), preferred_element_type=F32)


def dot_nt(a, b):
    return lax.dot_general(a, b, (((1,), (1,)), ((), ())), preferred_element_type=F32)


def kernel(
    len_ref, frames_h, w_in_h, w_dw, gain_ref, bias_ref, w_out_h, cot_h,
    out_h, gf_h, gwi_ref, gwo_ref, gk_ref, gg_ref, gb_ref,
    feats, w_in, w_out, cot, featsT, lin_v, sig_v, glu_p, dcv_p, conv_v, dsh_v,
    sw_v, swT, dpre_v, out_v, wb, vec,
    red, red_in, red_mid, red_rx1, red_rx2,
    gkl, kr1, ks1, kr2, kfull,
    wl, crx, cs, r1, s1, r2, s2, r3,
    in_sem, out_sem, halo_s, halo_r, ar1_s, ar1_r, ar2_s, ar2_r,
    k1_s, k1_r, k2_s, k2_r, k3_s, k3_r, rs_s, rs_r,
):
    dp = lax.axis_index("dp")
    tm = lax.axis_index("tm")
    z, x = dp // 4, dp % 4
    y, core = tm // 2, tm % 2
    pos = {"z": z, "x": x, "y": y}

    def at_axis(axis, p):
        if axis == "z":
            return (p * 4 + x, tm)
        if axis == "x":
            return (z * 4 + p, tm)
        return (dp, p * 2 + core)

    def rcopy(src, dst, ss, rs, dev):
        return pltpu.make_async_remote_copy(
            src_ref=src, dst_ref=dst, send_sem=ss, recv_sem=rs,
            device_id=dev, device_id_type=MESH_ID,
        )

    loads = [
        pltpu.make_async_copy(frames_h, feats, in_sem.at[0]),
        pltpu.make_async_copy(w_in_h, w_in, in_sem.at[1]),
        pltpu.make_async_copy(cot_h, cot, in_sem.at[2]),
        pltpu.make_async_copy(w_out_h, w_out, in_sem.at[3]),
    ]
    for c in loads:
        c.start()
    barrier = pltpu.get_barrier_semaphore()
    for d in range(1, NTM):
        pl.semaphore_signal(barrier, inc=1, device_id=(dp, (tm + d) % NTM), device_id_type=MESH_ID)
    for d in range(1, NDP):
        pl.semaphore_signal(barrier, inc=1, device_id=((dp + d) % NDP, tm), device_id_type=MESH_ID)

    limit = len_ref[0] - tm * ROWS

    def live_of(row0, rows, cols):
        t = lax.broadcasted_iota(jnp.int32, (rows, cols), 0) + row0
        return t < limit

    @pl.loop(0, TAPS)
    def _(k):
        row = w_dw[pl.ds(k, 1), :]
        for cb in range(CB):
            wb[cb, k + 1] = jnp.broadcast_to(row[:, cb * 128 : cb * 128 + 128], (8, 128))

    for ref in (glu_p, dcv_p):
        @pl.when(tm == 0)
        def _():
            ref[:, 0:PAD, :] = jnp.zeros((CB, PAD, 128), F32)

        @pl.when(tm == NTM - 1)
        def _():
            ref[:, PAD + ROWS : PROWS, :] = jnp.zeros((CB, PAD, 128), F32)

    loads[0].wait()
    loads[1].wait()

    @pl.loop(0, 4)
    def _(j):
        c0 = pl.multiple_of(j * 256, 256)

        @pl.loop(0, ROWS // MB)
        def _(m):
            r0 = pl.multiple_of(m * MB, MB)
            rows = feats[pl.ds(r0, MB), :]
            lin = dot_nn(rows, w_in[:, pl.ds(c0, 256)])
            sig = sigmoid(dot_nn(rows, w_in[:, pl.ds(CH + c0, 256)]))
            glu = jnp.where(live_of(r0, MB, 256), lin * sig, 0.0).astype(BF16).astype(F32)
            for h in range(2):
                cols = slice(h * 128, h * 128 + 128)
                lin_v[2 * j + h, pl.ds(r0, MB), :] = lin[:, cols]
                sig_v[2 * j + h, pl.ds(r0, MB), :] = sig[:, cols]
                glu_p[2 * j + h, pl.ds(PAD + r0, MB), :] = glu[:, cols]

    pl.semaphore_wait(barrier, NTM + NDP - 2)

    def halo(ref, n):
        to_left = rcopy(
            ref.at[:, pl.ds(PAD, PAD), :], ref.at[:, pl.ds(PAD + ROWS, PAD), :],
            halo_s.at[n], halo_r.at[n], (dp, (tm + NTM - 1) % NTM),
        )
        to_right = rcopy(
            ref.at[:, pl.ds(ROWS, PAD), :], ref.at[:, pl.ds(0, PAD), :],
            halo_s.at[n + 1], halo_r.at[n + 1], (dp, (tm + 1) % NTM),
        )

        def start():
            pl.when(tm > 0)(to_left.start)
            pl.when(tm < NTM - 1)(to_right.start)

        def recv():
            pl.when(tm < NTM - 1)(to_left.wait_recv)
            pl.when(tm > 0)(to_right.wait_recv)

        def sent():
            pl.when(tm > 0)(to_left.wait_send)
            pl.when(tm < NTM - 1)(to_right.wait_send)

        return start, recv, sent

    halo_g, halo_d = halo(glu_p, 0), halo(dcv_p, 2)
    halo_g[0]()

    loads[2].wait()
    loads[3].wait()

    @pl.loop(0, 4)
    def _(j):
        c0 = pl.multiple_of(j * 256, 256)

        @pl.loop(0, ROWS // MB)
        def _(m):
            r0 = pl.multiple_of(m * MB, MB)
            ds = dot_nt(cot[pl.ds(r0, MB), :], w_out[pl.ds(c0, 256), :])
            for h in range(2):
                dsh_v[2 * j + h, pl.ds(r0, MB), :] = ds[:, h * 128 : h * 128 + 128]

    def taps_pass(src, cb, row0, tap_of):
        acc = [None] * GRP
        for r in range(8):
            xs = [src[cb, pl.ds(row0 + (8 * n + r), 8), :] for n in range(GRP + 3)]
            for q in range(4):
                o = 8 * q + r
                if o == 0:
                    continue
                w = wb[cb, tap_of(o)]
                for g in range(GRP):
                    term = w * xs[g + q]
                    acc[g] = term if acc[g] is None else acc[g] + term
        return acc

    halo_g[1]()

    @pl.loop(0, CB)
    def _(cb):
        def step(i, carry):
            row0 = pl.multiple_of(i * (8 * GRP), 8 * GRP)
            s, sq = carry
            acc = taps_pass(glu_p, cb, row0, lambda o: o)
            for g in range(GRP):
                conv_v[cb, pl.ds(row0 + 8 * g, 8), :] = acc[g]
                kept = jnp.where(live_of(row0 + 8 * g, 8, 128), acc[g], 0.0)
                s = s + kept
                sq = sq + kept * kept
            return s, sq

        zero = jnp.zeros((8, 128), F32)
        s, sq = lax.fori_loop(0, GROUPS, step, (zero, zero))
        red[0, pl.ds(cb, 1), :] = jnp.sum(s, axis=0, keepdims=True)
        red[1, pl.ds(cb, 1), :] = jnp.sum(sq, axis=0, keepdims=True)

    def spread(axis, count, src_of, dst, ss, rs):
        me = tm if axis == "tm" else dp

        def copy(d, slot):
            peer = (me + d) % count
            dev = (dp, peer) if axis == "tm" else (peer, tm)
            return rcopy(src_of(peer), dst.at[slot], ss.at[d], rs.at[slot], dev)

        def start():
            for d in range(1, count):
                copy(d, me).start()

        def recv():
            for d in range(1, count):
                copy(d, (me + d) % count).wait_recv()

        def sent():
            for d in range(1, count):
                copy(d, me).wait_send()

        return start, recv, sent

    def total(ref, count):
        acc = ref[0]
        for i in range(1, count):
            acc = acc + ref[i]
        return acc

    def all_sum(n):
        one = spread("tm", NTM, lambda p: red_in.at[n], red_rx1.at[n], ar1_s.at[n], ar1_r.at[n])
        two = spread("dp", NDP, lambda p: red_mid.at[n], red_rx2.at[n], ar2_s.at[n], ar2_r.at[n])

        def begin():
            v = red[...]
            red_in[n] = v
            red_rx1[n, tm] = v
            one[0]()

        def middle():
            one[1]()
            v = total(red_rx1.at[n], NTM)
            red_mid[n] = v
            red_rx2[n, dp] = v
            two[0]()

        def end():
            two[1]()
            return total(red_rx2.at[n], NDP)

        def sent():
            one[2]()
            two[2]()

        return begin, middle, end, sent

    ar_a, ar_b = all_sum(0), all_sum(1)
    ar_a[0]()

    @pl.loop(0, 4)
    def _(i):
        c0 = pl.multiple_of(i * 256, 256)
        featsT[pl.ds(c0, 256), :] = feats[:, pl.ds(c0, 256)].T

    ar_a[1]()
    sums = ar_a[2]()
    mean = sums[0] * (1.0 / COUNT)
    variance = sums[1] * (1.0 / COUNT) - mean * mean
    inv_std = lax.rsqrt(variance + 1e-05)
    vec[0] = mean
    vec[1] = inv_std
    vec[2] = gain_ref[...]
    vec[3] = bias_ref[...]

    @pl.loop(0, CB)
    def _(cb):
        mean_r = vec[0, pl.ds(cb, 1), :]
        inv_r = vec[1, pl.ds(cb, 1), :]
        gain_r = vec[2, pl.ds(cb, 1), :]
        bias_r = vec[3, pl.ds(cb, 1), :]

        def step(i, carry):
            sg, sb = carry
            n = 64
            row0 = pl.multiple_of(i * n, n)
            live = live_of(row0, n, 128)
            normed = (conv_v[cb, pl.ds(row0, n), :] - mean_r) * inv_r
            shifted = gain_r * normed + bias_r
            act = sigmoid(shifted)
            sw_v[cb, pl.ds(row0, n), :] = jnp.where(live, shifted * act, 0.0).astype(BF16)
            slope = act * (1.0 + shifted * (1.0 - act))
            dsh = jnp.where(live, dsh_v[cb, pl.ds(row0, n), :] * slope, 0.0)
            dsh_v[cb, pl.ds(row0, n), :] = dsh
            conv_v[cb, pl.ds(row0, n), :] = normed
            prod = dsh * normed
            for g in range(n // 8):
                sg = sg + prod[8 * g : 8 * g + 8]
                sb = sb + dsh[8 * g : 8 * g + 8]
            return sg, sb

        zero = jnp.zeros((8, 128), F32)
        sg, sb = lax.fori_loop(0, ROWS // 64, step, (zero, zero))
        red[0, pl.ds(cb, 1), :] = jnp.sum(sg, axis=0, keepdims=True)
        red[1, pl.ds(cb, 1), :] = jnp.sum(sb, axis=0, keepdims=True)

    ar_b[0]()

    @pl.loop(0, ROWS // MB)
    def _(m):
        r0 = pl.multiple_of(m * MB, MB)
        rows = jnp.concatenate([sw_v[cb, pl.ds(r0, MB), :] for cb in range(CB)], axis=1)

        @pl.loop(0, 4)
        def _(j):
            c0 = pl.multiple_of(j * 256, 256)
            out_v[0, pl.ds(r0, MB), pl.ds(c0, 256)] = dot_nn(rows, w_out[:, pl.ds(c0, 256)]).astype(BF16)

    out_copy = pltpu.make_async_copy(out_v.at[0], out_h, out_sem.at[0])
    out_copy.start()
    ar_b[1]()

    def put_terms(b, i, first, second):
        both = jnp.concatenate(
            [first.reshape(16, 2, 8, 256), second.reshape(16, 2, 8, 256)], axis=2
        )
        wl[b, pl.ds(16 * i, 16)] = both.astype(BF16)

    def rs_core(b):
        return rcopy(
            wl.at[b, :, 1 - core], crx.at[b], rs_s.at[b, 0], rs_r.at[b, 0],
            (dp, tm + 1 - 2 * core),
        )

    def part_of(ref, dims, axis, p):
        at = dims.index(axis)
        return ref.at[tuple(slice(None) for _ in range(at)) + (p,)]

    def rs_copies(b, stage):
        order = ORDERS[b % 3]
        dims = ("z", "x", "y")
        src, dst = ((cs, r1), (s1, r2), (s2, r3))[stage]
        dims = tuple(a for a in dims if a not in order[:stage])
        axis = order[stage]
        copies = []
        for d in range(1, 4):
            p = (pos[axis] + d) % 4
            copies.append(
                rcopy(
                    part_of(src.at[b], dims, axis, p), dst.at[b, d - 1],
                    rs_s.at[b, 3 * stage + d], rs_r.at[b, 3 * stage + d], at_axis(axis, p),
                )
            )
        own = part_of(src.at[b], dims, axis, pos[axis])
        return copies, own, dst.at[b]

    def rs_one(b):
        rs_core(b).wait_recv()

        @pl.loop(0, 4)
        def _(i):
            rows = pl.ds(i * 16, 16)
            both = wl[b, rows, core].astype(F32) + crx[b, rows].astype(F32)
            cs[b, i] = both.astype(BF16).reshape(4, 4, 16, 256)

        for c in rs_copies(b, 0)[0]:
            c.start()

    def rs_next(b, stage):
        copies, own, got = rs_copies(b, stage)
        for c in copies:
            c.wait_recv()
        acc = own[...].astype(F32)
        for d in range(3):
            acc = acc + got[d].astype(F32)
        if stage < 2:
            (s1, s2)[stage][b] = acc.astype(BF16)
            for c in rs_copies(b, stage + 1)[0]:
                c.start()
        else:
            acc = acc * SCALE
            if b < 2:
                gwo_ref[:, 512 * b : 512 * b + 256] = acc[0:8]
                gwo_ref[:, 512 * b + 256 : 512 * b + 512] = acc[8:16]
            else:
                j = b - 2
                gwi_ref[:, 256 * j : 256 * j + 256] = acc[0:8]
                gwi_ref[:, CH + 256 * j : CH + 256 * j + 256] = acc[8:16]

    @pl.loop(0, 4)
    def _(i):
        for h in range(2):
            swT[pl.ds(256 * i + 128 * h, 128), :] = sw_v[2 * i + h].T

    for b in range(2):
        @pl.loop(0, 4)
        def _(i):
            rows = swT[pl.ds(pl.multiple_of(256 * i, 256), 256), :]
            put_terms(
                b, i,
                dot_nn(rows, cot[:, 512 * b : 512 * b + 256]),
                dot_nn(rows, cot[:, 512 * b + 256 : 512 * b + 512]),
            )

        rs_core(b).start()

    grads = ar_b[2]()
    gg_ref[...] = grads[0] * SCALE
    gb_ref[...] = grads[1] * SCALE
    vec[4] = gain_ref[...] * vec[1]
    vec[5] = grads[1] * (1.0 / COUNT)
    vec[6] = grads[0] * (1.0 / COUNT)

    @pl.loop(0, CB)
    def _(cb):
        factor = vec[4, pl.ds(cb, 1), :]
        shift = vec[5, pl.ds(cb, 1), :]
        tilt = vec[6, pl.ds(cb, 1), :]

        @pl.loop(0, ROWS // 64)
        def _(i):
            n = 64
            row0 = pl.multiple_of(i * n, n)
            inner = dsh_v[cb, pl.ds(row0, n), :] - shift - conv_v[cb, pl.ds(row0, n), :] * tilt
            dcv = jnp.where(live_of(row0, n, 128), factor * inner, 0.0)
            dcv_p[cb, pl.ds(PAD + row0, n), :] = dcv.astype(BF16).astype(F32)

    halo_d[0]()
    rs_one(0)
    rs_one(1)

    @pl.loop(0, CB)
    def _(cb):
        def step(i, accs):
            row0 = pl.multiple_of(i * (8 * GRP), 8 * GRP)
            accs = list(accs)
            ds = [dcv_p[cb, pl.ds(row0 + PAD + 8 * g, 8), :] for g in range(GRP)]
            for r in range(8):
                xs = [glu_p[cb, pl.ds(row0 + (8 * n + r), 8), :] for n in range(GRP + 3)]
                for q in range(4):
                    o = 8 * q + r
                    if o == 0:
                        continue
                    for g in range(GRP):
                        accs[o - 1] = accs[o - 1] + xs[g + q] * ds[g]
            return tuple(accs)

        zero = jnp.zeros((8, 128), F32)
        accs = lax.fori_loop(0, GROUPS, step, (zero,) * TAPS)
        for k in range(TAPS):
            gkl[k, pl.ds(cb, 1), :] = jnp.sum(accs[k], axis=0, keepdims=True)

    gkl[TAPS] = jnp.zeros((8, 128), F32)

    kt1 = spread("tm", NTM, lambda p: gkl.at[pl.ds(4 * p, 4)], kr1, k1_s, k1_r)
    kt2 = spread("dp", NDP, lambda p: ks1.at[0], kr2, k2_s, k2_r)
    kt3 = spread("tm", NTM, lambda p: ks1.at[1], kfull, k3_s, k3_r)
    kr1[tm] = gkl[pl.ds(4 * tm, 4)]
    kt1[0]()
    halo_d[1]()

    def back_block(j):
        b = 2 + j
        for h in range(2):
            cb = 2 * j + h

            @pl.loop(0, GROUPS)
            def _(i):
                row0 = pl.multiple_of(i * (8 * GRP), 8 * GRP)
                acc = taps_pass(dcv_p, cb, row0, lambda o: 32 - o)
                for g in range(0, GRP, 2):
                    dl, dg = [], []
                    for e in (g, g + 1):
                        rows = pl.ds(row0 + 8 * e, 8)
                        dglu = jnp.where(live_of(row0 + 8 * e, 8, 128), acc[e], 0.0)
                        sig = sig_v[cb, rows, :]
                        half = dglu * sig
                        dl.append(half)
                        dg.append(half * lin_v[cb, rows, :] * (1.0 - sig))
                    rows = pl.ds(row0 + 8 * g, 16)
                    dpre_v[cb, rows, :] = jnp.concatenate(dl, axis=0).astype(BF16)
                    dpre_v[CB + cb, rows, :] = jnp.concatenate(dg, axis=0).astype(BF16)

        first = jnp.concatenate([dpre_v[2 * j], dpre_v[2 * j + 1]], axis=1)
        second = jnp.concatenate([dpre_v[CB + 2 * j], dpre_v[CB + 2 * j + 1]], axis=1)

        @pl.loop(0, 4)
        def _(i):
            rows = featsT[pl.ds(pl.multiple_of(256 * i, 256), 256), :]
            put_terms(b, i, dot_nn(rows, first), dot_nn(rows, second))

        rs_core(b).start()

    back_block(0)
    rs_next(0, 0)
    rs_next(1, 0)
    kt1[1]()
    v = total(kr1, NTM)
    ks1[0] = v
    kr2[dp] = v
    kt2[0]()
    back_block(1)
    rs_one(2)
    rs_next(0, 1)
    rs_next(1, 1)
    kt2[1]()
    v = total(kr2, NDP)
    ks1[1] = v
    kfull[tm] = v
    kt3[0]()
    back_block(2)
    rs_one(3)
    rs_next(2, 0)
    rs_next(0, 2)
    rs_next(1, 2)
    kt3[1]()
    for cb in range(CB):
        for k in range(TAPS):
            gk_ref[k : k + 1, 128 * cb : 128 * cb + 128] = kfull[k // 4, k % 4, cb : cb + 1, :] * SCALE
    back_block(3)
    rs_one(4)
    rs_next(3, 0)
    rs_next(2, 1)

    def frame_rows(m):
        r0 = MB * m
        rows = jnp.concatenate([dpre_v[c, pl.ds(r0, MB), :] for c in range(2 * CB)], axis=1)

        @pl.loop(0, 4)
        def _(j):
            c0 = pl.multiple_of(j * 256, 256)
            out_v[1, pl.ds(r0, MB), pl.ds(c0, 256)] = dot_nt(rows, w_in[pl.ds(c0, 256), :]).astype(BF16)

    frame_rows(0)
    rs_one(5)
    rs_next(4, 0)
    rs_next(3, 1)
    rs_next(2, 2)
    frame_rows(1)
    rs_next(5, 0)
    rs_next(4, 1)
    rs_next(3, 2)
    frame_rows(2)
    gf_copy = pltpu.make_async_copy(out_v.at[1], gf_h, out_sem.at[1])
    gf_copy.start()
    rs_next(5, 1)
    rs_next(4, 2)
    rs_next(5, 2)

    for t in (halo_g, halo_d, kt1, kt2, kt3):
        t[2]()
    ar_a[3]()
    ar_b[3]()
    for b in range(NB):
        rs_core(b).wait_send()
        for stage in range(3):
            for c in rs_copies(b, stage)[0]:
                c.wait_send()
    out_copy.wait()
    gf_copy.wait()


SCALE = 1.0 / math.sqrt(16 * 6144)


def local(frames, lengths, w_in, w_dw, bn_gain, bn_bias, w_out, cotangent):
    hbm = pl.BlockSpec(memory_space=pl.ANY)
    vmem = pl.BlockSpec(memory_space=pltpu.VMEM)
    smem = pl.BlockSpec(memory_space=pltpu.SMEM)
    dma = pltpu.SemaphoreType.DMA
    outs = pl.pallas_call(
        kernel,
        out_shape=(
            jax.ShapeDtypeStruct((ROWS, CH), BF16),
            jax.ShapeDtypeStruct((ROWS, CH), BF16),
            jax.ShapeDtypeStruct((8, 2 * CH), F32),
            jax.ShapeDtypeStruct((8, CH), F32),
            jax.ShapeDtypeStruct((TAPS, CH), F32),
            jax.ShapeDtypeStruct((8, 128), F32),
            jax.ShapeDtypeStruct((8, 128), F32),
        ),
        in_specs=[smem, hbm, hbm, vmem, vmem, vmem, hbm, hbm],
        out_specs=(hbm, hbm, vmem, vmem, vmem, vmem, vmem),
        scratch_shapes=[
            pltpu.VMEM((ROWS, CH), BF16),
            pltpu.VMEM((CH, 2 * CH), BF16),
            pltpu.VMEM((CH, CH), BF16),
            pltpu.VMEM((ROWS, CH), BF16),
            pltpu.VMEM((CH, ROWS), BF16),
            pltpu.VMEM((CB, ROWS, 128), F32),
            pltpu.VMEM((CB, ROWS, 128), F32),
            pltpu.VMEM((CB, PROWS, 128), F32),
            pltpu.VMEM((CB, PROWS, 128), F32),
            pltpu.VMEM((CB, ROWS, 128), F32),
            pltpu.VMEM((CB, ROWS, 128), F32),
            pltpu.VMEM((CB, ROWS, 128), BF16),
            pltpu.VMEM((CH, ROWS), BF16),
            pltpu.VMEM((2 * CB, ROWS, 128), BF16),
            pltpu.VMEM((2, ROWS, CH), BF16),
            pltpu.VMEM((CB, 32, 8, 128), F32),
            pltpu.VMEM((8, 8, 128), F32),
            pltpu.VMEM((2, 8, 128), F32),
            pltpu.VMEM((2, 2, 8, 128), F32),
            pltpu.VMEM((2, 2, 8, 128), F32),
            pltpu.VMEM((2, NTM, 2, 8, 128), F32),
            pltpu.VMEM((2, NDP, 2, 8, 128), F32),
            pltpu.VMEM((32, 8, 128), F32),
            pltpu.VMEM((NTM, 4, 8, 128), F32),
            pltpu.VMEM((2, 4, 8, 128), F32),
            pltpu.VMEM((NDP, 4, 8, 128), F32),
            pltpu.VMEM((NTM, 4, 8, 128), F32),
            pltpu.VMEM((NB, 64, 2, 16, 256), BF16),
            pltpu.VMEM((NB, 64, 16, 256), BF16),
            pltpu.VMEM((NB, 4, 4, 4, 16, 256), BF16),
            pltpu.VMEM((NB, 3, 4, 4, 16, 256), BF16),
            pltpu.VMEM((NB, 4, 4, 16, 256), BF16),
            pltpu.VMEM((NB, 3, 4, 16, 256), BF16),
            pltpu.VMEM((NB, 4, 16, 256), BF16),
            pltpu.VMEM((NB, 3, 16, 256), BF16),
            dma((4,)),
            dma((2,)),
            dma((4,)),
            dma((4,)),
            dma((2, NTM)),
            dma((2, NTM)),
            dma((2, NDP)),
            dma((2, NDP)),
            dma((NTM,)),
            dma((NTM,)),
            dma((NDP,)),
            dma((NDP,)),
            dma((NTM,)),
            dma((NTM,)),
            dma((NB, 10)),
            dma((NB, 10)),
        ],
        compiler_params=pltpu.CompilerParams(
            collective_id=0, has_side_effects=True, vmem_limit_bytes=62 << 20
        ),
        name="conformer_conv",
    )(
        lengths, frames[0], w_in, w_dw, bn_gain.reshape(8, 128), bn_bias.reshape(8, 128),
        w_out, cotangent[0],
    )
    out, gf, gwi, gwo, gk, gg, gb = outs
    return (out[None], gf[None], gwi, gwo, gk, gg.reshape(CH), gb.reshape(CH))


def solution(mesh):
    placed = (P("dp", "tm", None), P("dp"), P(), P(), P(), P(), P(), P("dp", "tm", None))
    return jax.shard_map(
        local,
        mesh=mesh,
        in_specs=placed,
        out_specs=(
            P("dp", "tm", None),
            P("dp", "tm", None),
            P(("dp", "tm"), None),
            P(("dp", "tm"), None),
            P(),
            P(),
            P(),
        ),
        check_vma=False,
    )
```

```python
import math

import jax
import jax.numpy as jnp
from jax import lax
from jax.experimental import pallas as pl
from jax.experimental.pallas import tpu as pltpu
from jax.sharding import PartitionSpec as P

MESH_ID = pl.DeviceIdType.MESH
F32 = jnp.float32
BF16 = jnp.bfloat16

ROWS = 768
CH = 1024
CB = 8
PAD = 16
PROWS = ROWS + 2 * PAD
TAPS = 31
COUNT = 58982.0
NDP, NTM = 16, 8
GRP = 12
GROUPS = ROWS // (8 * GRP)
NB = 5
ORDERS = (("z", "x", "y"), ("x", "y", "z"), ("y", "z", "x"))


def sigmoid(x):
    return 0.5 * jnp.tanh(0.5 * x) + 0.5


def dot_nn(a, b):
    return lax.dot_general(a, b, (((1,), (0,)), ((), ())), preferred_element_type=F32)


def dot_nt(a, b):
    return lax.dot_general(a, b, (((1,), (1,)), ((), ())), preferred_element_type=F32)


def kernel(
    len_ref, frames_h, w_in_h, w_dw, gain_ref, bias_ref, w_out_h, cot_h,
    out_h, gf_h, gwi_ref, gwo_ref, gk_ref, gg_ref, gb_ref,
    feats, w_in, w_out, cot, featsT, stat_v, lin_v, sig_v, glu_p, dcv_p, conv_v, dsh_v,
    sw_v, swT, dpre_v, out_v, wb, vec,
    red, red_in, red_mid, red_rx1, red_rx2,
    gkl, kr1, ks1, kr2, kfull,
    wl_a, crx_a, cs_a, r1_a, s1_a, r2_a, s2_a, r3_a,
    wl_b, crx_b, cs_b, r1_b, s1_b, r2_b, s2_b, r3_b,
    in_sem, w_sem, out_sem, halo_s, halo_r, ar1_s, ar1_r, ar2_s, ar2_r,
    k1_s, k1_r, k2_s, k2_r, k3_s, k3_r, rs_s, rs_r,
):
    dp = lax.axis_index("dp")
    tm = lax.axis_index("tm")
    z, x = dp // 4, dp % 4
    y, core = tm // 2, tm % 2
    pos = {"z": z, "x": x, "y": y}

    def at_axis(axis, p):
        if axis == "z":
            return (p * 4 + x, tm)
        if axis == "x":
            return (z * 4 + p, tm)
        return (dp, p * 2 + core)

    def rcopy(src, dst, ss, rs, dev):
        return pltpu.make_async_remote_copy(
            src_ref=src, dst_ref=dst, send_sem=ss, recv_sem=rs,
            device_id=dev, device_id_type=MESH_ID,
        )

    def w_in_load(j, half):
        cols = pl.ds(half * CH + j * 256, 256)
        return pltpu.make_async_copy(w_in_h.at[:, cols], w_in.at[:, cols], w_sem.at[j, half])

    loads = [
        pltpu.make_async_copy(frames_h, feats, in_sem.at[0]),
        pltpu.make_async_copy(cot_h, cot, in_sem.at[1]),
        pltpu.make_async_copy(w_out_h, w_out, in_sem.at[2]),
    ]
    loads[0].start()
    for j in range(4):
        for half in range(2):
            w_in_load(j, half).start()
    loads[1].start()
    loads[2].start()
    barrier = pltpu.get_barrier_semaphore()
    for d in range(1, NTM):
        pl.semaphore_signal(barrier, inc=1, device_id=(dp, (tm + d) % NTM), device_id_type=MESH_ID)
    for d in range(1, NDP):
        pl.semaphore_signal(barrier, inc=1, device_id=((dp + d) % NDP, tm), device_id_type=MESH_ID)

    limit = len_ref[0] - tm * ROWS

    def live_of(row0, rows, cols):
        t = lax.broadcasted_iota(jnp.int32, (rows, cols), 0) + row0
        return t < limit

    @pl.loop(0, TAPS)
    def _(k):
        row = w_dw[pl.ds(k, 1), :]
        for cb in range(CB):
            wb[cb, k + 1] = jnp.broadcast_to(row[:, cb * 128 : cb * 128 + 128], (8, 128))

    for ref in (glu_p, dcv_p):
        @pl.when(tm == 0)
        def _():
            ref[:, 0:PAD, :] = jnp.zeros((CB, PAD, 128), F32)

        @pl.when(tm == NTM - 1)
        def _():
            ref[:, PAD + ROWS : PROWS, :] = jnp.zeros((CB, PAD, 128), F32)

    loads[0].wait()

    @pl.loop(0, 4)
    def _(j):
        c0 = pl.multiple_of(j * 256, 256)
        w_in_load(j, 0).wait()
        w_in_load(j, 1).wait()
        rows = feats[...]
        lin = dot_nn(rows, w_in[:, pl.ds(c0, 256)])
        sig = sigmoid(dot_nn(rows, w_in[:, pl.ds(CH + c0, 256)]))
        glu = jnp.where(live_of(0, ROWS, 256), lin * sig, 0.0).astype(BF16).astype(F32)
        for h in range(2):
            cols = slice(h * 128, h * 128 + 128)
            lin_v[2 * j + h] = lin[:, cols]
            sig_v[2 * j + h] = sig[:, cols]
            glu_p[2 * j + h, pl.ds(PAD, ROWS), :] = glu[:, cols]

    def halo(ref, n):
        to_left = rcopy(
            ref.at[:, pl.ds(PAD, PAD), :], ref.at[:, pl.ds(PAD + ROWS, PAD), :],
            halo_s.at[n], halo_r.at[n], (dp, (tm + NTM - 1) % NTM),
        )
        to_right = rcopy(
            ref.at[:, pl.ds(ROWS, PAD), :], ref.at[:, pl.ds(0, PAD), :],
            halo_s.at[n + 1], halo_r.at[n + 1], (dp, (tm + 1) % NTM),
        )

        def start():
            pl.when(tm > 0)(to_left.start)
            pl.when(tm < NTM - 1)(to_right.start)

        def recv():
            pl.when(tm < NTM - 1)(to_left.wait_recv)
            pl.when(tm > 0)(to_right.wait_recv)

        def sent():
            pl.when(tm > 0)(to_left.wait_send)
            pl.when(tm < NTM - 1)(to_right.wait_send)

        return start, recv, sent

    halo_g, halo_d = halo(glu_p, 0), halo(dcv_p, 2)
    def taps_pass(src, cb, row0, tap_of, grp):
        acc = [None] * grp
        for r in range(8):
            xs = [src[cb, pl.ds(row0 + (8 * n + r), 8), :] for n in range(grp + 3)]
            for q in range(4):
                o = 8 * q + r
                if o == 0:
                    continue
                w = wb[cb, tap_of(o)]
                for g in range(grp):
                    term = w * xs[g + q]
                    acc[g] = term if acc[g] is None else acc[g] + term
        return acc

    def conv_rows(cb, row0, grp, carry):
        s, sq = carry
        acc = taps_pass(glu_p, cb, row0, lambda o: o, grp)
        for g in range(grp):
            conv_v[cb, pl.ds(row0 + 8 * g, 8), :] = acc[g]
            kept = jnp.where(live_of(row0 + 8 * g, 8, 128), acc[g], 0.0)
            s = s + kept
            sq = sq + kept * kept
        return s, sq

    EDGE, INNER = 8, 16

    def conv_inner(cb):
        def step(i, carry):
            return conv_rows(cb, pl.multiple_of(64 + i * 128, 64), INNER, carry)

        zero = jnp.zeros((8, 128), F32)
        s, sq = lax.fori_loop(0, (ROWS - 128) // 128, step, (zero, zero))
        stat_v[cb, 0] = s
        stat_v[cb, 1] = sq

    pl.loop(0, 2)(conv_inner)
    pl.semaphore_wait(barrier, NTM + NDP - 2)
    halo_g[0]()
    pl.loop(2, CB)(conv_inner)
    halo_g[1]()

    @pl.loop(0, CB)
    def _(cb):
        def step(i, carry):
            return conv_rows(cb, pl.multiple_of(i * (ROWS - 64), 64), EDGE, carry)

        s, sq = lax.fori_loop(0, 2, step, (stat_v[cb, 0], stat_v[cb, 1]))
        red[0, pl.ds(cb, 1), :] = jnp.sum(s, axis=0, keepdims=True)
        red[1, pl.ds(cb, 1), :] = jnp.sum(sq, axis=0, keepdims=True)

    def spread(axis, count, src_of, dst, ss, rs):
        me = tm if axis == "tm" else dp

        def copy(d, slot):
            peer = (me + d) % count
            dev = (dp, peer) if axis == "tm" else (peer, tm)
            return rcopy(src_of(peer), dst.at[slot], ss.at[d], rs.at[slot], dev)

        def start():
            for d in range(1, count):
                copy(d, me).start()

        def recv():
            for d in range(1, count):
                copy(d, (me + d) % count).wait_recv()

        def sent():
            for d in range(1, count):
                copy(d, me).wait_send()

        return start, recv, sent

    def total(ref, count):
        acc = ref[0]
        for i in range(1, count):
            acc = acc + ref[i]
        return acc

    def all_sum(n):
        one = spread("tm", NTM, lambda p: red_in.at[n], red_rx1.at[n], ar1_s.at[n], ar1_r.at[n])
        two = spread("dp", NDP, lambda p: red_mid.at[n], red_rx2.at[n], ar2_s.at[n], ar2_r.at[n])

        def begin():
            v = red[...]
            red_in[n] = v
            red_rx1[n, tm] = v
            one[0]()

        def middle():
            one[1]()
            v = total(red_rx1.at[n], NTM)
            red_mid[n] = v
            red_rx2[n, dp] = v
            two[0]()

        def end():
            two[1]()
            return total(red_rx2.at[n], NDP)

        def sent():
            one[2]()
            two[2]()

        return begin, middle, end, sent

    ar_a, ar_b = all_sum(0), all_sum(1)
    ar_a[0]()

    loads[1].wait()
    loads[2].wait()

    @pl.loop(0, 4)
    def _(j):
        c0 = pl.multiple_of(j * 256, 256)
        ds = dot_nt(cot[...], w_out[pl.ds(c0, 256), :])
        for h in range(2):
            dsh_v[2 * j + h] = ds[:, h * 128 : h * 128 + 128]

    @pl.loop(0, 4)
    def _(i):
        c0 = pl.multiple_of(i * 256, 256)
        featsT[pl.ds(c0, 256), :] = feats[:, pl.ds(c0, 256)].T

    ar_a[1]()
    sums = ar_a[2]()
    mean = sums[0] * (1.0 / COUNT)
    variance = sums[1] * (1.0 / COUNT) - mean * mean
    inv_std = lax.rsqrt(variance + 1e-05)
    vec[0] = mean
    vec[1] = inv_std
    vec[2] = gain_ref[...]
    vec[3] = bias_ref[...]

    @pl.loop(0, CB)
    def _(cb):
        mean_r = vec[0, pl.ds(cb, 1), :]
        inv_r = vec[1, pl.ds(cb, 1), :]
        gain_r = vec[2, pl.ds(cb, 1), :]
        bias_r = vec[3, pl.ds(cb, 1), :]

        def step(i, carry):
            sg, sb = carry
            n = 256
            row0 = pl.multiple_of(i * n, n)
            live = live_of(row0, n, 128)
            normed = (conv_v[cb, pl.ds(row0, n), :] - mean_r) * inv_r
            shifted = gain_r * normed + bias_r
            act = sigmoid(shifted)
            sw_v[cb, pl.ds(row0, n), :] = jnp.where(live, shifted * act, 0.0).astype(BF16)
            slope = act * (1.0 + shifted * (1.0 - act))
            dsh = jnp.where(live, dsh_v[cb, pl.ds(row0, n), :] * slope, 0.0)
            dsh_v[cb, pl.ds(row0, n), :] = dsh
            conv_v[cb, pl.ds(row0, n), :] = normed
            prod = dsh * normed
            for g in range(n // 8):
                sg = sg + prod[8 * g : 8 * g + 8]
                sb = sb + dsh[8 * g : 8 * g + 8]
            return sg, sb

        zero = jnp.zeros((8, 128), F32)
        sg, sb = lax.fori_loop(0, ROWS // 256, step, (zero, zero))
        red[0, pl.ds(cb, 1), :] = jnp.sum(sg, axis=0, keepdims=True)
        red[1, pl.ds(cb, 1), :] = jnp.sum(sb, axis=0, keepdims=True)

    ar_b[0]()

    def buf(name, b):
        first, rest = rs_bufs[name]
        return first if b == 0 else rest.at[b - 1]

    rs_bufs = {
        "wl": (wl_a, wl_b), "crx": (crx_a, crx_b), "cs": (cs_a, cs_b),
        "r1": (r1_a, r1_b), "s1": (s1_a, s1_b), "r2": (r2_a, r2_b),
        "s2": (s2_a, s2_b), "r3": (r3_a, r3_b),
    }

    def put_terms(dst, rows, cols, first, second):
        n = first.shape[0] // 16
        both = jnp.concatenate(
            [first.reshape(n, 2, 8, 256), second.reshape(n, 2, 8, 256)], axis=2
        )
        dst[pl.ds(n * rows, n), :, :, cols] = both.astype(BF16)

    def rs_core(b):
        return rcopy(
            buf("wl", b).at[:, 1 - core], buf("crx", b), rs_s.at[b, 0], rs_r.at[b, 0],
            (dp, tm + 1 - 2 * core),
        )

    def part_of(ref, dims, axis, p):
        at = dims.index(axis)
        return ref.at[tuple(slice(None) for _ in range(at)) + (p,)]

    def rs_copies(b, stage):
        order = ORDERS[b % 3]
        dims = ("z", "x", "y")
        src, dst = (("cs", "r1"), ("s1", "r2"), ("s2", "r3"))[stage]
        src, dst = buf(src, b), buf(dst, b)
        dims = tuple(a for a in dims if a not in order[:stage])
        axis = order[stage]
        copies = []
        for d in range(1, 4):
            p = (pos[axis] + d) % 4
            copies.append(
                rcopy(
                    part_of(src, dims, axis, p), dst.at[d - 1],
                    rs_s.at[b, 3 * stage + d], rs_r.at[b, 3 * stage + d], at_axis(axis, p),
                )
            )
        own = part_of(src, dims, axis, pos[axis])
        return copies, own, dst

    def rs_one(b):
        rs_core(b).wait_recv()

        @pl.loop(0, 4)
        def _(i):
            rows = pl.ds(i * 16, 16)
            both = buf("wl", b)[rows, core].astype(F32) + buf("crx", b)[rows].astype(F32)
            buf("cs", b)[i] = both.astype(BF16).reshape(4, 4, 16, both.shape[-1])

        for c in rs_copies(b, 0)[0]:
            c.start()

    def rs_next(b, stage):
        copies, own, got = rs_copies(b, stage)
        for c in copies:
            c.wait_recv()
        acc = own[...].astype(F32)
        for d in range(3):
            acc = acc + got[d].astype(F32)
        if stage < 2:
            buf(("s1", "s2")[stage], b)[...] = acc.astype(BF16)
            for c in rs_copies(b, stage + 1)[0]:
                c.start()
        else:
            acc = acc * SCALE
            if b == 0:
                gwo_ref[:, 0:512] = acc[0:8]
                gwo_ref[:, 512:1024] = acc[8:16]
            else:
                j = b - 1
                gwi_ref[:, 256 * j : 256 * j + 256] = acc[0:8]
                gwi_ref[:, CH + 256 * j : CH + 256 * j + 256] = acc[8:16]

    @pl.loop(0, 4)
    def _(i):
        for h in range(2):
            swT[pl.ds(256 * i + 128 * h, 128), :] = sw_v[2 * i + h].T

    for half in range(2):
        cols = slice(256 * half, 256 * half + 256)

        @pl.loop(0, 2)
        def _(i):
            rows = swT[pl.ds(pl.multiple_of(512 * i, 512), 512), :]
            put_terms(
                wl_a, i, cols,
                dot_nn(rows, cot[:, 256 * half : 256 * half + 256]),
                dot_nn(rows, cot[:, 512 + 256 * half : 512 + 256 * half + 256]),
            )

    rs_core(0).start()
    ar_b[1]()

    @pl.loop(0, 4)
    def _(j):
        c0 = pl.multiple_of(j * 256, 256)
        rows = jnp.concatenate([sw_v[cb] for cb in range(CB)], axis=1)
        out_v[0, :, pl.ds(c0, 256)] = dot_nn(rows, w_out[:, pl.ds(c0, 256)]).astype(BF16)

    out_copy = pltpu.make_async_copy(out_v.at[0], out_h, out_sem.at[0])
    out_copy.start()
    rs_one(0)

    grads = ar_b[2]()
    gg_ref[...] = grads[0] * SCALE
    gb_ref[...] = grads[1] * SCALE
    vec[4] = gain_ref[...] * vec[1]
    vec[5] = grads[1] * (1.0 / COUNT)
    vec[6] = grads[0] * (1.0 / COUNT)

    @pl.loop(0, CB)
    def _(cb):
        factor = vec[4, pl.ds(cb, 1), :]
        shift = vec[5, pl.ds(cb, 1), :]
        tilt = vec[6, pl.ds(cb, 1), :]

        @pl.loop(0, ROWS // 256)
        def _(i):
            n = 256
            row0 = pl.multiple_of(i * n, n)
            inner = dsh_v[cb, pl.ds(row0, n), :] - shift - conv_v[cb, pl.ds(row0, n), :] * tilt
            dcv = jnp.where(live_of(row0, n, 128), factor * inner, 0.0)
            dcv_p[cb, pl.ds(PAD + row0, n), :] = dcv.astype(BF16).astype(F32)

    halo_d[0]()

    def kernel_grad(cb):
        def step(i, accs):
            row0 = pl.multiple_of(i * (8 * GRP), 8 * GRP)
            accs = list(accs)
            ds = [dcv_p[cb, pl.ds(row0 + PAD + 8 * g, 8), :] for g in range(GRP)]
            for r in range(8):
                xs = [glu_p[cb, pl.ds(row0 + (8 * n + r), 8), :] for n in range(GRP + 3)]
                for q in range(4):
                    o = 8 * q + r
                    if o == 0:
                        continue
                    for g in range(GRP):
                        accs[o - 1] = accs[o - 1] + xs[g + q] * ds[g]
            return tuple(accs)

        zero = jnp.zeros((8, 128), F32)
        accs = lax.fori_loop(0, GROUPS, step, (zero,) * TAPS)
        for k in range(TAPS):
            gkl[k, pl.ds(cb, 1), :] = jnp.sum(accs[k], axis=0, keepdims=True)

    gkl[TAPS] = jnp.zeros((8, 128), F32)
    pl.loop(0, 5)(kernel_grad)

    kt1 = spread("tm", NTM, lambda p: gkl.at[pl.ds(4 * p, 4)], kr1, k1_s, k1_r)
    kt2 = spread("dp", NDP, lambda p: ks1.at[0], kr2, k2_s, k2_r)
    kt3 = spread("tm", NTM, lambda p: ks1.at[1], kfull, k3_s, k3_r)
    halo_d[1]()

    def back_block(j):
        b = 1 + j
        for h in range(2):
            cb = 2 * j + h

            @pl.loop(0, GROUPS)
            def _(i):
                row0 = pl.multiple_of(i * (8 * GRP), 8 * GRP)
                acc = taps_pass(dcv_p, cb, row0, lambda o: 32 - o, GRP)
                for g in range(0, GRP, 2):
                    dl, dg = [], []
                    for e in (g, g + 1):
                        rows = pl.ds(row0 + 8 * e, 8)
                        dglu = jnp.where(live_of(row0 + 8 * e, 8, 128), acc[e], 0.0)
                        sig = sig_v[cb, rows, :]
                        half = dglu * sig
                        dl.append(half)
                        dg.append(half * lin_v[cb, rows, :] * (1.0 - sig))
                    rows = pl.ds(row0 + 8 * g, 16)
                    dpre_v[cb, rows, :] = jnp.concatenate(dl, axis=0).astype(BF16)
                    dpre_v[CB + cb, rows, :] = jnp.concatenate(dg, axis=0).astype(BF16)

        first = jnp.concatenate([dpre_v[2 * j], dpre_v[2 * j + 1]], axis=1)
        second = jnp.concatenate([dpre_v[CB + 2 * j], dpre_v[CB + 2 * j + 1]], axis=1)

        @pl.loop(0, 2)
        def _(i):
            rows = featsT[pl.ds(pl.multiple_of(512 * i, 512), 512), :]
            put_terms(buf("wl", b), i, slice(None), dot_nn(rows, first), dot_nn(rows, second))

        rs_core(b).start()

    def kt_sum(n):
        if n == 0:
            kr1[tm] = gkl[pl.ds(4 * tm, 4)]
            kt1[0]()
        elif n == 1:
            kt1[1]()
            v = total(kr1, NTM)
            ks1[0] = v
            kr2[dp] = v
            kt2[0]()
        elif n == 2:
            kt2[1]()
            v = total(kr2, NDP)
            ks1[1] = v
            kfull[tm] = v
            kt3[0]()
        else:
            kt3[1]()
            for cb in range(CB):
                for k in range(TAPS):
                    row = kfull[k // 4, k % 4, cb : cb + 1, :]
                    gk_ref[k : k + 1, 128 * cb : 128 * cb + 128] = row * SCALE

    def frame_cols(j):
        rows = jnp.concatenate([dpre_v[c] for c in range(2 * CB)], axis=1)
        part = dot_nt(rows, w_in[256 * j : 256 * j + 256, :])
        out_v[1, :, 256 * j : 256 * j + 256] = part.astype(BF16)

    back_block(0)
    back_block(1)
    rs_one(1)
    rs_next(0, 0)
    back_block(2)
    rs_one(2)
    rs_next(0, 1)
    back_block(3)
    rs_one(3)
    rs_next(1, 0)
    pl.loop(5, CB)(kernel_grad)
    kt_sum(0)
    rs_one(4)
    rs_next(0, 2)
    rs_next(2, 0)

    frame_cols(0)
    rs_next(1, 1)
    frame_cols(1)
    rs_next(3, 0)
    frame_cols(2)
    kt_sum(1)
    frame_cols(3)
    gf_copy = pltpu.make_async_copy(out_v.at[1], gf_h, out_sem.at[1])
    gf_copy.start()
    rs_next(2, 1)
    rs_next(1, 2)
    rs_next(4, 0)
    rs_next(3, 1)
    kt_sum(2)
    rs_next(2, 2)
    rs_next(4, 1)
    rs_next(3, 2)
    kt_sum(3)
    rs_next(4, 2)

    for t in (halo_g, halo_d, kt1, kt2, kt3):
        t[2]()
    ar_a[3]()
    ar_b[3]()
    for b in range(NB):
        rs_core(b).wait_send()
        for stage in range(3):
            for c in rs_copies(b, stage)[0]:
                c.wait_send()
    out_copy.wait()
    gf_copy.wait()


SCALE = 1.0 / math.sqrt(16 * 6144)


def rs_scratch(lead, width):
    shapes = (
        (64, 2), (64,), (4, 4, 4), (3, 4, 4), (4, 4), (3, 4), (4,), (3,),
    )
    return [pltpu.VMEM((*lead, *s, 16, width), BF16) for s in shapes]


PIECES = ((0, 4), (1, 4), (2, 1), (3, 1), (4, 1), (5, 1), (6, 1))


def hand_over(*refs):
    srcs, dsts, held, sems = refs[0:7], refs[7:14], refs[14:21], refs[21]
    steps = []
    for i, parts in PIECES:
        rows = srcs[i].shape[0] // parts
        for p in range(parts):
            at = (pl.ds(p * rows, rows),)
            n = len(steps)
            steps.append((
                pltpu.make_async_copy(srcs[i].at[at], held[i].at[at], sems.at[n, 0]),
                pltpu.make_async_copy(held[i].at[at], dsts[i].at[at], sems.at[n, 1]),
            ))
    for come, _ in steps:
        come.start()
    for come, go in steps:
        come.wait()
        go.start()
    for _, go in steps:
        go.wait()


def local(frames, lengths, w_in, w_dw, bn_gain, bn_bias, w_out, cotangent):
    hbm = pl.BlockSpec(memory_space=pl.ANY)
    vmem = pl.BlockSpec(memory_space=pltpu.VMEM)
    smem = pl.BlockSpec(memory_space=pltpu.SMEM)
    dma = pltpu.SemaphoreType.DMA
    outs = pl.pallas_call(
        kernel,
        out_shape=(
            jax.ShapeDtypeStruct((ROWS, CH), BF16),
            jax.ShapeDtypeStruct((ROWS, CH), BF16),
            jax.ShapeDtypeStruct((8, 2 * CH), F32),
            jax.ShapeDtypeStruct((8, CH), F32),
            jax.ShapeDtypeStruct((TAPS, CH), F32),
            jax.ShapeDtypeStruct((8, 128), F32),
            jax.ShapeDtypeStruct((8, 128), F32),
        ),
        in_specs=[smem, hbm, hbm, vmem, vmem, vmem, hbm, hbm],
        out_specs=(hbm, hbm, vmem, vmem, vmem, vmem, vmem),
        scratch_shapes=[
            pltpu.VMEM((ROWS, CH), BF16),
            pltpu.VMEM((CH, 2 * CH), BF16),
            pltpu.VMEM((CH, CH), BF16),
            pltpu.VMEM((ROWS, CH), BF16),
            pltpu.VMEM((CH, ROWS), BF16),
            pltpu.VMEM((CB, 2, 8, 128), F32),
            pltpu.VMEM((CB, ROWS, 128), F32),
            pltpu.VMEM((CB, ROWS, 128), F32),
            pltpu.VMEM((CB, PROWS, 128), F32),
            pltpu.VMEM((CB, PROWS, 128), F32),
            pltpu.VMEM((CB, ROWS, 128), F32),
            pltpu.VMEM((CB, ROWS, 128), F32),
            pltpu.VMEM((CB, ROWS, 128), BF16),
            pltpu.VMEM((CH, ROWS), BF16),
            pltpu.VMEM((2 * CB, ROWS, 128), BF16),
            pltpu.VMEM((2, ROWS, CH), BF16),
            pltpu.VMEM((CB, 32, 8, 128), F32),
            pltpu.VMEM((8, 8, 128), F32),
            pltpu.VMEM((2, 8, 128), F32),
            pltpu.VMEM((2, 2, 8, 128), F32),
            pltpu.VMEM((2, 2, 8, 128), F32),
            pltpu.VMEM((2, NTM, 2, 8, 128), F32),
            pltpu.VMEM((2, NDP, 2, 8, 128), F32),
            pltpu.VMEM((32, 8, 128), F32),
            pltpu.VMEM((NTM, 4, 8, 128), F32),
            pltpu.VMEM((2, 4, 8, 128), F32),
            pltpu.VMEM((NDP, 4, 8, 128), F32),
            pltpu.VMEM((NTM, 4, 8, 128), F32),
            *rs_scratch((), 512),
            *rs_scratch((NB - 1,), 256),
            dma((3,)),
            dma((4, 2)),
            dma((2,)),
            dma((4,)),
            dma((4,)),
            dma((2, NTM)),
            dma((2, NTM)),
            dma((2, NDP)),
            dma((2, NDP)),
            dma((NTM,)),
            dma((NTM,)),
            dma((NDP,)),
            dma((NDP,)),
            dma((NTM,)),
            dma((NTM,)),
            dma((NB, 10)),
            dma((NB, 10)),
        ],
        compiler_params=pltpu.CompilerParams(
            collective_id=0, has_side_effects=True, vmem_limit_bytes=62 << 20
        ),
        name="conformer_conv",
    )(
        lengths, frames[0], w_in, w_dw, bn_gain.reshape(8, 128), bn_bias.reshape(8, 128),
        w_out, cotangent[0],
    )
    out, gf, gwi, gwo, gk, gg, gb = pl.pallas_call(
        hand_over,
        out_shape=tuple(jax.ShapeDtypeStruct(o.shape, o.dtype) for o in outs),
        in_specs=[hbm] * 7,
        out_specs=(hbm,) * 7,
        scratch_shapes=[pltpu.VMEM(o.shape, o.dtype) for o in outs] + [dma((13, 2))],
        name="hand_over",
    )(*outs)
    return (out[None], gf[None], gwi, gwo, gk, gg.reshape(CH), gb.reshape(CH))


def solution(mesh):
    placed = (P("dp", "tm", None), P("dp"), P(), P(), P(), P(), P(), P("dp", "tm", None))
    return jax.shard_map(
        local,
        mesh=mesh,
        in_specs=placed,
        out_specs=(
            P("dp", "tm", None),
            P("dp", "tm", None),
            P(("dp", "tm"), None),
            P(("dp", "tm"), None),
            P(),
            P(),
            P(),
        ),
        check_vma=False,
    )
```

```python
import math

import jax
import jax.numpy as jnp
from jax import lax
from jax.experimental import pallas as pl
from jax.experimental.pallas import tpu as pltpu
from jax.sharding import PartitionSpec as P

MESH_ID = pl.DeviceIdType.MESH
F32 = jnp.float32
BF16 = jnp.bfloat16

ROWS = 768
CH = 1024
CB = 8
PAD = 16
PROWS = ROWS + 2 * PAD
TAPS = 31
COUNT = 58982.0
NDP, NTM = 16, 8
GRP = 12
GROUPS = ROWS // (8 * GRP)
NB = 6
ORDERS = (("z", "x", "y"), ("x", "y", "z"), ("y", "z", "x"))


def sigmoid(x):
    return 0.5 * jnp.tanh(0.5 * x) + 0.5


def dot_nn(a, b):
    return lax.dot_general(a, b, (((1,), (0,)), ((), ())), preferred_element_type=F32)


def dot_nt(a, b):
    return lax.dot_general(a, b, (((1,), (1,)), ((), ())), preferred_element_type=F32)


def kernel(
    len_ref, frames_h, w_in_h, w_dw, gain_ref, bias_ref, w_out_h, cot_h,
    out_h, gf_h, gwi_ref, gwo_ref, gk_ref, gg_ref, gb_ref,
    feats, w_in, w_out, cot, featsT, stat_v, lin_v, sig_v, glu_p, dcv_p, conv_v, dsh_v,
    sw_v, swT, dpre_v, out_v, wb, vec,
    red, red_in, red_mid, red_rx1, red_rx2,
    gkl, gk1, gk2, gk3, kr1, ks1, kr2, kfull,
    wl_a, crx_a, cs_a, r1_a, s1_a, r2_a, s2_a, r3_a,
    wl_b, crx_b, cs_b, r1_b, s1_b, r2_b, s2_b, r3_b,
    wl_c, crx_c, cs_c, r1_c, s1_c, r2_c, s2_c, r3_c,
    in_sem, w_sem, out_sem, halo_s, halo_r, ar1_s, ar1_r, ar2_s, ar2_r,
    k1_s, k1_r, k2_s, k2_r, k3_s, k3_r, rs_s, rs_r,
):
    dp = lax.axis_index("dp")
    tm = lax.axis_index("tm")
    z, x = dp // 4, dp % 4
    y, core = tm // 2, tm % 2
    pos = {"z": z, "x": x, "y": y}

    def at_axis(axis, p):
        if axis == "z":
            return (p * 4 + x, tm)
        if axis == "x":
            return (z * 4 + p, tm)
        return (dp, p * 2 + core)

    def rcopy(src, dst, ss, rs, dev):
        return pltpu.make_async_remote_copy(
            src_ref=src, dst_ref=dst, send_sem=ss, recv_sem=rs,
            device_id=dev, device_id_type=MESH_ID,
        )

    def w_in_load(j, half):
        cols = pl.ds(half * CH + j * 256, 256)
        return pltpu.make_async_copy(w_in_h.at[:, cols], w_in.at[:, cols], w_sem.at[j, half])

    loads = [
        pltpu.make_async_copy(frames_h, feats, in_sem.at[0]),
        pltpu.make_async_copy(cot_h, cot, in_sem.at[1]),
        pltpu.make_async_copy(w_out_h, w_out, in_sem.at[2]),
    ]
    loads[0].start()
    for j in range(4):
        for half in range(2):
            w_in_load(j, half).start()
    loads[1].start()
    loads[2].start()
    barrier = pltpu.get_barrier_semaphore()
    for d in range(1, NTM):
        pl.semaphore_signal(barrier, inc=1, device_id=(dp, (tm + d) % NTM), device_id_type=MESH_ID)
    for d in range(1, NDP):
        pl.semaphore_signal(barrier, inc=1, device_id=((dp + d) % NDP, tm), device_id_type=MESH_ID)

    limit = len_ref[0] - tm * ROWS

    def live_of(row0, rows, cols):
        t = lax.broadcasted_iota(jnp.int32, (rows, cols), 0) + row0
        return t < limit

    @pl.loop(0, TAPS)
    def _(k):
        row = w_dw[pl.ds(k, 1), :]
        for cb in range(CB):
            wb[cb, k + 1] = jnp.broadcast_to(row[:, cb * 128 : cb * 128 + 128], (8, 128))

    for ref in (glu_p, dcv_p):
        @pl.when(tm == 0)
        def _():
            ref[:, 0:PAD, :] = jnp.zeros((CB, PAD, 128), F32)

        @pl.when(tm == NTM - 1)
        def _():
            ref[:, PAD + ROWS : PROWS, :] = jnp.zeros((CB, PAD, 128), F32)

    loads[0].wait()

    @pl.loop(0, 4)
    def _(j):
        c0 = pl.multiple_of(j * 256, 256)
        w_in_load(j, 0).wait()
        w_in_load(j, 1).wait()
        rows = feats[...]
        lin = dot_nn(rows, w_in[:, pl.ds(c0, 256)])
        sig = sigmoid(dot_nn(rows, w_in[:, pl.ds(CH + c0, 256)]))
        glu = jnp.where(live_of(0, ROWS, 256), lin * sig, 0.0).astype(BF16).astype(F32)
        for h in range(2):
            cols = slice(h * 128, h * 128 + 128)
            lin_v[2 * j + h] = lin[:, cols]
            sig_v[2 * j + h] = sig[:, cols]
            glu_p[2 * j + h, pl.ds(PAD, ROWS), :] = glu[:, cols]

    def halo(ref, n):
        to_left = rcopy(
            ref.at[:, pl.ds(PAD, PAD), :], ref.at[:, pl.ds(PAD + ROWS, PAD), :],
            halo_s.at[n], halo_r.at[n], (dp, (tm + NTM - 1) % NTM),
        )
        to_right = rcopy(
            ref.at[:, pl.ds(ROWS, PAD), :], ref.at[:, pl.ds(0, PAD), :],
            halo_s.at[n + 1], halo_r.at[n + 1], (dp, (tm + 1) % NTM),
        )

        def start():
            pl.when(tm > 0)(to_left.start)
            pl.when(tm < NTM - 1)(to_right.start)

        def recv():
            pl.when(tm < NTM - 1)(to_left.wait_recv)
            pl.when(tm > 0)(to_right.wait_recv)

        def sent():
            pl.when(tm > 0)(to_left.wait_send)
            pl.when(tm < NTM - 1)(to_right.wait_send)

        return start, recv, sent

    halo_g, halo_d = halo(glu_p, 0), halo(dcv_p, 2)
    def taps_pass(src, cb, row0, tap_of, grp):
        acc = [None] * grp
        for r in range(8):
            xs = [src[cb, pl.ds(row0 + (8 * n + r), 8), :] for n in range(grp + 3)]
            for q in range(4):
                o = 8 * q + r
                if o == 0:
                    continue
                w = wb[cb, tap_of(o)]
                for g in range(grp):
                    term = w * xs[g + q]
                    acc[g] = term if acc[g] is None else acc[g] + term
        return acc

    def conv_rows(cb, row0, grp, carry):
        s, sq = carry
        acc = taps_pass(glu_p, cb, row0, lambda o: o, grp)
        for g in range(grp):
            kept = jnp.where(live_of(row0 + 8 * g, 8, 128), acc[g], 0.0)
            conv_v[cb, pl.ds(row0 + 8 * g, 8), :] = kept
            s = s + kept
            sq = sq + kept * kept
        return s, sq

    EDGE, INNER = 8, 16

    def conv_inner(cb):
        s = sq = jnp.zeros((8, 128), F32)
        for i in range((ROWS - 128) // 128):
            s, sq = conv_rows(cb, 64 + i * 128, INNER, (s, sq))
        stat_v[cb, 0] = s
        stat_v[cb, 1] = sq

    pl.loop(0, 2)(conv_inner)
    pl.semaphore_wait(barrier, NTM + NDP - 2)
    halo_g[0]()
    pl.loop(2, CB)(conv_inner)
    halo_g[1]()

    @pl.loop(0, CB)
    def _(cb):
        s, sq = stat_v[cb, 0], stat_v[cb, 1]
        for row0 in (0, ROWS - 64):
            s, sq = conv_rows(cb, row0, EDGE, (s, sq))
        red[0, pl.ds(cb, 1), :] = jnp.sum(s, axis=0, keepdims=True)
        red[1, pl.ds(cb, 1), :] = jnp.sum(sq, axis=0, keepdims=True)

    def spread(axis, count, src_of, dst, ss, rs):
        me = tm if axis == "tm" else dp

        def copy(d, slot):
            peer = (me + d) % count
            dev = (dp, peer) if axis == "tm" else (peer, tm)
            return rcopy(src_of(peer), dst.at[slot], ss.at[d], rs.at[slot], dev)

        def start():
            for d in range(1, count):
                copy(d, me).start()

        def recv():
            for d in range(1, count):
                copy(d, (me + d) % count).wait_recv()

        def sent():
            for d in range(1, count):
                copy(d, me).wait_send()

        return start, recv, sent

    def total(ref, count):
        acc = ref[0]
        for i in range(1, count):
            acc = acc + ref[i]
        return acc

    def all_sum(n):
        one = spread("tm", NTM, lambda p: red_in.at[n], red_rx1.at[n], ar1_s.at[n], ar1_r.at[n])
        two = spread("dp", NDP, lambda p: red_mid.at[n], red_rx2.at[n], ar2_s.at[n], ar2_r.at[n])

        def begin():
            v = red[...]
            red_in[n] = v
            red_rx1[n, tm] = v
            one[0]()

        def middle():
            one[1]()
            v = total(red_rx1.at[n], NTM)
            red_mid[n] = v
            red_rx2[n, dp] = v
            two[0]()

        def end():
            two[1]()
            return total(red_rx2.at[n], NDP)

        def sent():
            one[2]()
            two[2]()

        return begin, middle, end, sent

    ar_a, ar_b = all_sum(0), all_sum(1)
    ar_a[0]()

    loads[1].wait()
    loads[2].wait()

    @pl.loop(0, 4)
    def _(j):
        c0 = pl.multiple_of(j * 256, 256)
        ds = dot_nt(cot[...], w_out[pl.ds(c0, 256), :])
        for h in range(2):
            dsh_v[2 * j + h] = ds[:, h * 128 : h * 128 + 128]

    @pl.loop(0, 4)
    def _(i):
        c0 = pl.multiple_of(i * 256, 256)
        featsT[pl.ds(c0, 256), :] = feats[:, pl.ds(c0, 256)].T

    def tap_sums(dst, grad):
        grp = 16

        @pl.loop(0, CB)
        def _(cb):
            def step(i, accs):
                row0 = pl.multiple_of(i * (8 * grp), 8 * grp)
                accs = list(accs)
                ds = [grad[cb, pl.ds(row0 + 8 * g, 8), :] for g in range(grp)]
                for r in range(8):
                    xs = [glu_p[cb, pl.ds(row0 + (8 * n + r), 8), :] for n in range(grp + 3)]
                    for q in range(4):
                        o = 8 * q + r
                        if o == 0:
                            continue
                        for g in range(grp):
                            accs[o - 1] = accs[o - 1] + xs[g + q] * ds[g]
                return tuple(accs)

            zero = jnp.zeros((8, 128), F32)
            accs = lax.fori_loop(0, ROWS // (8 * grp), step, (zero,) * TAPS)
            for k in range(TAPS):
                dst[k + 1, pl.ds(cb, 1), :] = jnp.sum(accs[k], axis=0, keepdims=True)

    def window(rows_of):
        count = jnp.clip(limit, 0, ROWS)
        row, tap = rows_of
        return ((row >= tap) & (row < count + tap)).astype(F32).astype(BF16)

    def live_sums():
        def grid(n):
            return [lax.broadcasted_iota(jnp.int32, (32, n), d) for d in (1, 0)]

        row, tap = grid(ROWS)
        inner = window((row + PAD, tap))
        row, tap = grid(2 * PAD)
        outer = window((jnp.where(row < PAD, row, row + ROWS), tap))
        for cb in range(CB):
            ends = jnp.concatenate(
                [glu_p[cb, 0:PAD, :], glu_p[cb, PAD + ROWS : PROWS, :]], axis=0
            )
            gk2[:, cb, :] = dot_nn(inner, glu_p[cb, PAD : PAD + ROWS, :].astype(BF16)) + dot_nn(
                outer, ends.astype(BF16)
            )

    ar_a[1]()
    live_sums()
    tap_sums(gk3, conv_v)
    sums = ar_a[2]()
    mean = sums[0] * (1.0 / COUNT)
    variance = sums[1] * (1.0 / COUNT) - mean * mean
    inv_std = lax.rsqrt(variance + 1e-05)
    vec[0] = mean
    vec[1] = inv_std
    vec[2] = gain_ref[...]
    vec[3] = bias_ref[...]

    @pl.loop(0, CB)
    def _(cb):
        mean_r = vec[0, pl.ds(cb, 1), :]
        inv_r = vec[1, pl.ds(cb, 1), :]
        gain_r = vec[2, pl.ds(cb, 1), :]
        bias_r = vec[3, pl.ds(cb, 1), :]

        def step(i, carry):
            sg, sb = carry
            n = 256
            row0 = pl.multiple_of(i * n, n)
            live = live_of(row0, n, 128)
            normed = (conv_v[cb, pl.ds(row0, n), :] - mean_r) * inv_r
            shifted = gain_r * normed + bias_r
            act = sigmoid(shifted)
            sw_v[cb, pl.ds(row0, n), :] = jnp.where(live, shifted * act, 0.0).astype(BF16)
            slope = act * (1.0 + shifted * (1.0 - act))
            dsh = jnp.where(live, dsh_v[cb, pl.ds(row0, n), :] * slope, 0.0)
            dsh_v[cb, pl.ds(row0, n), :] = dsh
            conv_v[cb, pl.ds(row0, n), :] = normed
            prod = dsh * normed
            for g in range(n // 8):
                sg = sg + prod[8 * g : 8 * g + 8]
                sb = sb + dsh[8 * g : 8 * g + 8]
            return sg, sb

        zero = jnp.zeros((8, 128), F32)
        sg, sb = lax.fori_loop(0, ROWS // 256, step, (zero, zero))
        red[0, pl.ds(cb, 1), :] = jnp.sum(sg, axis=0, keepdims=True)
        red[1, pl.ds(cb, 1), :] = jnp.sum(sb, axis=0, keepdims=True)

    ar_b[0]()

    def buf(name, b):
        whole, pairs, singles = rs_bufs[name]
        return whole if b == 0 else pairs.at[b - 1] if b < 4 else singles.at[b - 4]

    rs_bufs = {
        "wl": (wl_a, wl_b, wl_c), "crx": (crx_a, crx_b, crx_c), "cs": (cs_a, cs_b, cs_c),
        "r1": (r1_a, r1_b, r1_c), "s1": (s1_a, s1_b, s1_c), "r2": (r2_a, r2_b, r2_c),
        "s2": (s2_a, s2_b, s2_c), "r3": (r3_a, r3_b, r3_c),
    }

    def put_terms(dst, rows, cols, first, second):
        n, w = first.shape[0] // 16, first.shape[1]
        both = jnp.concatenate([first.reshape(n, 2, 8, w), second.reshape(n, 2, 8, w)], axis=2)
        dst[pl.ds(n * rows, n), :, :, cols] = both.astype(BF16)

    def rs_core(b):
        return rcopy(
            buf("wl", b).at[:, 1 - core], buf("crx", b), rs_s.at[b, 0], rs_r.at[b, 0],
            (dp, tm + 1 - 2 * core),
        )

    def part_of(ref, dims, axis, p):
        at = dims.index(axis)
        return ref.at[tuple(slice(None) for _ in range(at)) + (p,)]

    def rs_copies(b, stage):
        order = ORDERS[b % 3]
        dims = ("z", "x", "y")
        src, dst = (("cs", "r1"), ("s1", "r2"), ("s2", "r3"))[stage]
        src, dst = buf(src, b), buf(dst, b)
        dims = tuple(a for a in dims if a not in order[:stage])
        axis = order[stage]
        copies = []
        for d in range(1, 4):
            p = (pos[axis] + d) % 4
            copies.append(
                rcopy(
                    part_of(src, dims, axis, p), dst.at[d - 1],
                    rs_s.at[b, 3 * stage + d], rs_r.at[b, 3 * stage + d], at_axis(axis, p),
                )
            )
        own = part_of(src, dims, axis, pos[axis])
        return copies, own, dst

    def rs_one(b):
        rs_core(b).wait_recv()

        @pl.loop(0, 4)
        def _(i):
            rows = pl.ds(i * 16, 16)
            both = buf("wl", b)[rows, core].astype(F32) + buf("crx", b)[rows].astype(F32)
            buf("cs", b)[i] = both.astype(BF16).reshape(4, 4, 16, both.shape[-1])

        for c in rs_copies(b, 0)[0]:
            c.start()

    def rs_next(b, stage):
        copies, own, got = rs_copies(b, stage)
        for c in copies:
            c.wait_recv()
        acc = own[...].astype(F32)
        for d in range(3):
            acc = acc + got[d].astype(F32)
        if stage < 2:
            buf(("s1", "s2")[stage], b)[...] = acc.astype(BF16)
            for c in rs_copies(b, stage + 1)[0]:
                c.start()
        else:
            acc = acc * SCALE
            if b == 0:
                gwo_ref[:, 0:512] = acc[0:8]
                gwo_ref[:, 512:1024] = acc[8:16]
            else:
                c0, w = (256 * (b - 1), 256) if b < 4 else (128 * (b + 2), 128)
                gwi_ref[:, c0 : c0 + w] = acc[0:8]
                gwi_ref[:, CH + c0 : CH + c0 + w] = acc[8:16]

    @pl.loop(0, 4)
    def _(i):
        for h in range(2):
            swT[pl.ds(256 * i + 128 * h, 128), :] = sw_v[2 * i + h].T

    for half in range(2):
        cols = slice(256 * half, 256 * half + 256)

        @pl.loop(0, 2)
        def _(i):
            rows = swT[pl.ds(pl.multiple_of(512 * i, 512), 512), :]
            put_terms(
                wl_a, i, cols,
                dot_nn(rows, cot[:, 256 * half : 256 * half + 256]),
                dot_nn(rows, cot[:, 512 + 256 * half : 512 + 256 * half + 256]),
            )

    rs_core(0).start()
    ar_b[1]()

    tap_sums(gk1, dsh_v)
    rs_one(0)

    grads = ar_b[2]()
    gg_ref[...] = grads[0] * SCALE
    gb_ref[...] = grads[1] * SCALE
    vec[4] = gain_ref[...] * vec[1]
    vec[5] = grads[1] * (1.0 / COUNT)
    vec[6] = grads[0] * (1.0 / COUNT)

    def dconv_rows(parts):
        @pl.loop(0, CB)
        def _(cb):
            factor = vec[4, pl.ds(cb, 1), :]
            shift = vec[5, pl.ds(cb, 1), :]
            tilt = vec[6, pl.ds(cb, 1), :]
            for row0, n in parts:
                rows = pl.ds(row0, n)
                inner = dsh_v[cb, rows, :] - shift - conv_v[cb, rows, :] * tilt
                dcv = jnp.where(live_of(row0, n, 128), factor * inner, 0.0)
                dcv_p[cb, pl.ds(PAD + row0, n), :] = dcv.astype(BF16).astype(F32)

    dconv_rows(((0, PAD), (ROWS - PAD, PAD)))
    halo_d[0]()

    mean, inv_std = vec[0], vec[1]
    for o in range(1, TAPS + 1):
        tilted = inv_std * (gk3[o] - mean * gk2[o])
        gkl[o - 1] = vec[4] * (gk1[o] - vec[5] * gk2[o] - vec[6] * tilted)
    gkl[TAPS] = jnp.zeros((8, 128), F32)

    kt1 = spread("tm", NTM, lambda p: gkl.at[pl.ds(4 * p, 4)], kr1, k1_s, k1_r)
    kt2 = spread("dp", NDP, lambda p: ks1.at[0], kr2, k2_s, k2_r)
    kt3 = spread("tm", NTM, lambda p: ks1.at[1], kfull, k3_s, k3_r)
    def back_rows(cb, row0, grp):
        acc = taps_pass(dcv_p, cb, row0, lambda o: 32 - o, grp)
        for g in range(0, grp, 2):
            dl, dg = [], []
            for e in (g, g + 1):
                rows = pl.ds(row0 + 8 * e, 8)
                dglu = jnp.where(live_of(row0 + 8 * e, 8, 128), acc[e], 0.0)
                sig = sig_v[cb, rows, :]
                half = dglu * sig
                dl.append(half)
                dg.append(half * lin_v[cb, rows, :] * (1.0 - sig))
            rows = pl.ds(row0 + 8 * g, 16)
            dpre_v[cb, rows, :] = jnp.concatenate(dl, axis=0).astype(BF16)
            dpre_v[CB + cb, rows, :] = jnp.concatenate(dg, axis=0).astype(BF16)

    def back_inner(cb):
        for i in range((ROWS - 128) // 128):
            back_rows(cb, 64 + 128 * i, INNER)

    def back_edges(cb):
        for row0 in (0, ROWS - 64):
            back_rows(cb, row0, EDGE)

    def back_all(cb):
        for i in range(GROUPS):
            back_rows(cb, 8 * GRP * i, GRP)

    def pair_terms(j):
        first = jnp.concatenate([dpre_v[2 * j], dpre_v[2 * j + 1]], axis=1)
        second = jnp.concatenate([dpre_v[CB + 2 * j], dpre_v[CB + 2 * j + 1]], axis=1)

        @pl.loop(0, 2)
        def _(i):
            rows = featsT[pl.ds(pl.multiple_of(512 * i, 512), 512), :]
            put_terms(buf("wl", 1 + j), i, slice(None), dot_nn(rows, first), dot_nn(rows, second))

        rs_core(1 + j).start()

    def single_terms(b):
        cb = b + 2
        both = jnp.concatenate([dpre_v[cb], dpre_v[CB + cb]], axis=1)

        @pl.loop(0, 2)
        def _(i):
            rows = featsT[pl.ds(pl.multiple_of(512 * i, 512), 512), :]
            part = dot_nn(rows, both)
            put_terms(buf("wl", b), i, slice(None), part[:, 0:128], part[:, 128:256])

        rs_core(b).start()

    def kt_sum(n):
        if n == 0:
            kr1[tm] = gkl[pl.ds(4 * tm, 4)]
            kt1[0]()
        elif n == 1:
            kt1[1]()
            v = total(kr1, NTM)
            ks1[0] = v
            kr2[dp] = v
            kt2[0]()
        elif n == 2:
            kt2[1]()
            v = total(kr2, NDP)
            ks1[1] = v
            kfull[tm] = v
            kt3[0]()
        else:
            kt3[1]()
            for cb in range(CB):
                for k in range(TAPS):
                    row = kfull[k // 4, k % 4, cb : cb + 1, :]
                    gk_ref[k : k + 1, 128 * cb : 128 * cb + 128] = row * SCALE

    def frame_cols(j):
        rows = jnp.concatenate([dpre_v[c] for c in range(2 * CB)], axis=1)
        part = dot_nt(rows, w_in[256 * j : 256 * j + 256, :])
        out_v[1, :, 256 * j : 256 * j + 256] = part.astype(BF16)

    def out_cols(j):
        rows = jnp.concatenate([sw_v[cb] for cb in range(CB)], axis=1)
        part = dot_nn(rows, w_out[:, 256 * j : 256 * j + 256])
        out_v[0, :, 256 * j : 256 * j + 256] = part.astype(BF16)

    kt_sum(0)
    dconv_rows(((PAD, 384), (PAD + 384, 352)))
    pl.loop(0, 2)(back_inner)
    halo_d[1]()
    pl.loop(0, 2)(back_edges)
    pair_terms(0)
    kt_sum(1)
    pl.loop(2, 4)(back_all)
    pair_terms(1)
    rs_one(1)
    pl.loop(4, 6)(back_all)
    pair_terms(2)
    rs_one(2)
    kt_sum(2)
    rs_next(0, 0)
    pl.loop(6, 7)(back_all)
    single_terms(4)
    rs_one(3)
    pl.loop(7, 8)(back_all)
    single_terms(5)
    rs_one(4)

    frame_cols(0)
    rs_one(5)
    rs_next(1, 0)
    frame_cols(1)
    rs_next(0, 1)
    rs_next(2, 0)
    frame_cols(2)
    rs_next(3, 0)
    frame_cols(3)
    gf_copy = pltpu.make_async_copy(out_v.at[1], gf_h, out_sem.at[1])
    gf_copy.start()
    rs_next(4, 0)
    rs_next(1, 1)
    out_cols(0)
    out_cols(1)
    rs_next(5, 0)
    rs_next(2, 1)
    out_cols(2)
    out_cols(3)
    out_copy = pltpu.make_async_copy(out_v.at[0], out_h, out_sem.at[0])
    out_copy.start()
    rs_next(3, 1)
    rs_next(4, 1)
    rs_next(0, 2)
    kt_sum(3)
    rs_next(5, 1)
    rs_next(1, 2)
    rs_next(2, 2)
    rs_next(3, 2)
    rs_next(4, 2)
    rs_next(5, 2)

    for t in (halo_g, halo_d, kt1, kt2, kt3):
        t[2]()
    ar_a[3]()
    ar_b[3]()
    for b in range(NB):
        rs_core(b).wait_send()
        for stage in range(3):
            for c in rs_copies(b, stage)[0]:
                c.wait_send()
    out_copy.wait()
    gf_copy.wait()


SCALE = 1.0 / math.sqrt(16 * 6144)


def rs_scratch(lead, width):
    shapes = (
        (64, 2), (64,), (4, 4, 4), (3, 4, 4), (4, 4), (3, 4), (4,), (3,),
    )
    return [pltpu.VMEM((*lead, *s, 16, width), BF16) for s in shapes]


PIECES = ((0, 4), (1, 4), (2, 1), (3, 1), (4, 1), (5, 1), (6, 1))


def hand_over(*refs):
    srcs, dsts, held, sems = refs[0:7], refs[7:14], refs[14:21], refs[21]
    steps = []
    for i, parts in PIECES:
        rows = srcs[i].shape[0] // parts
        for p in range(parts):
            at = (pl.ds(p * rows, rows),)
            n = len(steps)
            steps.append((
                pltpu.make_async_copy(srcs[i].at[at], held[i].at[at], sems.at[n, 0]),
                pltpu.make_async_copy(held[i].at[at], dsts[i].at[at], sems.at[n, 1]),
            ))
    for come, _ in steps:
        come.start()
    for come, go in steps:
        come.wait()
        go.start()
    for _, go in steps:
        go.wait()


def local(frames, lengths, w_in, w_dw, bn_gain, bn_bias, w_out, cotangent):
    hbm = pl.BlockSpec(memory_space=pl.ANY)
    vmem = pl.BlockSpec(memory_space=pltpu.VMEM)
    smem = pl.BlockSpec(memory_space=pltpu.SMEM)
    dma = pltpu.SemaphoreType.DMA
    outs = pl.pallas_call(
        kernel,
        out_shape=(
            jax.ShapeDtypeStruct((ROWS, CH), BF16),
            jax.ShapeDtypeStruct((ROWS, CH), BF16),
            jax.ShapeDtypeStruct((8, 2 * CH), F32),
            jax.ShapeDtypeStruct((8, CH), F32),
            jax.ShapeDtypeStruct((TAPS, CH), F32),
            jax.ShapeDtypeStruct((8, 128), F32),
            jax.ShapeDtypeStruct((8, 128), F32),
        ),
        in_specs=[smem, hbm, hbm, vmem, vmem, vmem, hbm, hbm],
        out_specs=(hbm, hbm, vmem, vmem, vmem, vmem, vmem),
        scratch_shapes=[
            pltpu.VMEM((ROWS, CH), BF16),
            pltpu.VMEM((CH, 2 * CH), BF16),
            pltpu.VMEM((CH, CH), BF16),
            pltpu.VMEM((ROWS, CH), BF16),
            pltpu.VMEM((CH, ROWS), BF16),
            pltpu.VMEM((CB, 2, 8, 128), F32),
            pltpu.VMEM((CB, ROWS, 128), F32),
            pltpu.VMEM((CB, ROWS, 128), F32),
            pltpu.VMEM((CB, PROWS, 128), F32),
            pltpu.VMEM((CB, PROWS, 128), F32),
            pltpu.VMEM((CB, ROWS, 128), F32),
            pltpu.VMEM((CB, ROWS, 128), F32),
            pltpu.VMEM((CB, ROWS, 128), BF16),
            pltpu.VMEM((CH, ROWS), BF16),
            pltpu.VMEM((2 * CB, ROWS, 128), BF16),
            pltpu.VMEM((2, ROWS, CH), BF16),
            pltpu.VMEM((CB, 32, 8, 128), F32),
            pltpu.VMEM((8, 8, 128), F32),
            pltpu.VMEM((2, 8, 128), F32),
            pltpu.VMEM((2, 2, 8, 128), F32),
            pltpu.VMEM((2, 2, 8, 128), F32),
            pltpu.VMEM((2, NTM, 2, 8, 128), F32),
            pltpu.VMEM((2, NDP, 2, 8, 128), F32),
            pltpu.VMEM((32, 8, 128), F32),
            pltpu.VMEM((32, 8, 128), F32),
            pltpu.VMEM((32, 8, 128), F32),
            pltpu.VMEM((32, 8, 128), F32),
            pltpu.VMEM((NTM, 4, 8, 128), F32),
            pltpu.VMEM((2, 4, 8, 128), F32),
            pltpu.VMEM((NDP, 4, 8, 128), F32),
            pltpu.VMEM((NTM, 4, 8, 128), F32),
            *rs_scratch((), 512),
            *rs_scratch((3,), 256),
            *rs_scratch((2,), 128),
            dma((3,)),
            dma((4, 2)),
            dma((2,)),
            dma((4,)),
            dma((4,)),
            dma((2, NTM)),
            dma((2, NTM)),
            dma((2, NDP)),
            dma((2, NDP)),
            dma((NTM,)),
            dma((NTM,)),
            dma((NDP,)),
            dma((NDP,)),
            dma((NTM,)),
            dma((NTM,)),
            dma((NB, 10)),
            dma((NB, 10)),
        ],
        compiler_params=pltpu.CompilerParams(
            collective_id=0, has_side_effects=True, vmem_limit_bytes=62 << 20
        ),
        name="conformer_conv",
    )(
        lengths, frames[0], w_in, w_dw, bn_gain.reshape(8, 128), bn_bias.reshape(8, 128),
        w_out, cotangent[0],
    )
    out, gf, gwi, gwo, gk, gg, gb = pl.pallas_call(
        hand_over,
        out_shape=tuple(jax.ShapeDtypeStruct(o.shape, o.dtype) for o in outs),
        in_specs=[hbm] * 7,
        out_specs=(hbm,) * 7,
        scratch_shapes=[pltpu.VMEM(o.shape, o.dtype) for o in outs] + [dma((13, 2))],
        name="hand_over",
    )(*outs)
    return (out[None], gf[None], gwi, gwo, gk, gg.reshape(CH), gb.reshape(CH))


def solution(mesh):
    placed = (P("dp", "tm", None), P("dp"), P(), P(), P(), P(), P(), P("dp", "tm", None))
    return jax.shard_map(
        local,
        mesh=mesh,
        in_specs=placed,
        out_specs=(
            P("dp", "tm", None),
            P("dp", "tm", None),
            P(("dp", "tm"), None),
            P(("dp", "tm"), None),
            P(),
            P(),
            P(),
        ),
        check_vma=False,
    )
```

```python
import math

import jax
import jax.numpy as jnp
from jax import lax
from jax.experimental import pallas as pl
from jax.experimental.pallas import tpu as pltpu
from jax.sharding import PartitionSpec as P

MESH_ID = pl.DeviceIdType.MESH
F32 = jnp.float32
BF16 = jnp.bfloat16

ROWS = 768
CH = 1024
CB = 8
PAD = 16
PROWS = ROWS + 2 * PAD
TAPS = 31
COUNT = 58982.0
NDP, NTM = 16, 8
GRP = 12
GROUPS = ROWS // (8 * GRP)
NB = 6
ORDER = ("z", "x", "y")


def sigmoid(x):
    return 0.5 * jnp.tanh(0.5 * x) + 0.5


def dot_nn(a, b):
    return lax.dot_general(a, b, (((1,), (0,)), ((), ())), preferred_element_type=F32)


def dot_tn(a, b):
    return lax.dot_general(a, b, (((0,), (0,)), ((), ())), preferred_element_type=F32)


def dot_nt(a, b):
    return lax.dot_general(a, b, (((1,), (1,)), ((), ())), preferred_element_type=F32)


def kernel(
    len_ref, frames_h, w_in_h, w_dw, gain_ref, bias_ref, w_out_h, cot_h,
    out_h, gf_h, gwi_ref, gwo_ref, gk_ref, gg_ref, gb_ref,
    feats, w_in, w_out, cot, stat_v, lin_v, sig_v, glu_p, dcv_p, conv_v, dsh_v,
    sw_v, dpre_v, out_v, wb, vec,
    red, red_in, red_mid, red_rx1, red_rx2,
    gkl, gk1, gk2, gk3, kr1, ks1, kr2, ks2, kfull,
    wl_a, crx_a, cs_a, r1_a, s1_a, r2_a, s2_a, r3_a,
    wl_b, crx_b, cs_b, r1_b, s1_b, r2_b, s2_b, r3_b,
    wl_c, crx_c, cs_c, r1_c, s1_c, r2_c, s2_c, r3_c,
    in_sem, w_sem, out_sem, halo_s, halo_r, ar1_s, ar1_r, ar2_s, ar2_r,
    k1_s, k1_r, k2_s, k2_r, k3_s, k3_r, rs_s, rs_r,
):
    dp = lax.axis_index("dp")
    tm = lax.axis_index("tm")
    z, x = dp // 4, dp % 4
    y, core = tm // 2, tm % 2
    pos = {"z": z, "x": x, "y": y}

    def at_axis(axis, p):
        if axis == "z":
            return (p * 4 + x, tm)
        if axis == "x":
            return (z * 4 + p, tm)
        return (dp, p * 2 + core)

    def rcopy(src, dst, ss, rs, dev):
        return pltpu.make_async_remote_copy(
            src_ref=src, dst_ref=dst, send_sem=ss, recv_sem=rs,
            device_id=dev, device_id_type=MESH_ID,
        )

    def w_in_load(j, half):
        cols = pl.ds(half * CH + j * 256, 256)
        return pltpu.make_async_copy(w_in_h.at[:, cols], w_in.at[:, cols], w_sem.at[j, half])

    loads = [
        pltpu.make_async_copy(frames_h, feats, in_sem.at[0]),
        pltpu.make_async_copy(cot_h, cot, in_sem.at[1]),
        pltpu.make_async_copy(w_out_h, w_out, in_sem.at[2]),
    ]
    loads[0].start()
    for j in range(4):
        for half in range(2):
            w_in_load(j, half).start()
    loads[1].start()
    loads[2].start()
    barrier = pltpu.get_barrier_semaphore()
    for d in range(1, NTM):
        pl.semaphore_signal(barrier, inc=1, device_id=(dp, (tm + d) % NTM), device_id_type=MESH_ID)
    for d in range(1, NDP):
        pl.semaphore_signal(barrier, inc=1, device_id=((dp + d) % NDP, tm), device_id_type=MESH_ID)

    limit = len_ref[0] - tm * ROWS

    def live_of(row0, rows, cols):
        t = lax.broadcasted_iota(jnp.int32, (rows, cols), 0) + row0
        return t < limit

    @pl.loop(0, TAPS)
    def _(k):
        row = w_dw[pl.ds(k, 1), :]
        for cb in range(CB):
            wb[cb, k + 1] = jnp.broadcast_to(row[:, cb * 128 : cb * 128 + 128], (8, 128))

    for ref in (glu_p, dcv_p):
        @pl.when(tm == 0)
        def _():
            ref[:, 0:PAD, :] = jnp.zeros((CB, PAD, 128), F32)

        @pl.when(tm == NTM - 1)
        def _():
            ref[:, PAD + ROWS : PROWS, :] = jnp.zeros((CB, PAD, 128), F32)

    loads[0].wait()

    @pl.loop(0, 4)
    def _(j):
        c0 = pl.multiple_of(j * 256, 256)
        w_in_load(j, 0).wait()
        w_in_load(j, 1).wait()
        rows = feats[...]
        lin = dot_nn(rows, w_in[:, pl.ds(c0, 256)])
        sig = sigmoid(dot_nn(rows, w_in[:, pl.ds(CH + c0, 256)]))
        glu = jnp.where(live_of(0, ROWS, 256), lin * sig, 0.0).astype(BF16).astype(F32)
        for h in range(2):
            cols = slice(h * 128, h * 128 + 128)
            lin_v[2 * j + h] = lin[:, cols]
            sig_v[2 * j + h] = sig[:, cols]
            glu_p[2 * j + h, pl.ds(PAD, ROWS), :] = glu[:, cols]

    def halo(ref, n):
        to_left = rcopy(
            ref.at[:, pl.ds(PAD, PAD), :], ref.at[:, pl.ds(PAD + ROWS, PAD), :],
            halo_s.at[n], halo_r.at[n], (dp, (tm + NTM - 1) % NTM),
        )
        to_right = rcopy(
            ref.at[:, pl.ds(ROWS, PAD), :], ref.at[:, pl.ds(0, PAD), :],
            halo_s.at[n + 1], halo_r.at[n + 1], (dp, (tm + 1) % NTM),
        )

        def start():
            pl.when(tm > 0)(to_left.start)
            pl.when(tm < NTM - 1)(to_right.start)

        def recv():
            pl.when(tm < NTM - 1)(to_left.wait_recv)
            pl.when(tm > 0)(to_right.wait_recv)

        def sent():
            pl.when(tm > 0)(to_left.wait_send)
            pl.when(tm < NTM - 1)(to_right.wait_send)

        return start, recv, sent

    halo_g, halo_d = halo(glu_p, 0), halo(dcv_p, 2)
    def taps_pass(src, cb, row0, tap_of, grp):
        acc = [None] * grp
        for r in range(8):
            xs = [src[cb, pl.ds(row0 + (8 * n + r), 8), :] for n in range(grp + 3)]
            for q in range(4):
                o = 8 * q + r
                if o == 0:
                    continue
                w = wb[cb, tap_of(o)]
                for g in range(grp):
                    term = w * xs[g + q]
                    acc[g] = term if acc[g] is None else acc[g] + term
        return acc

    def conv_rows(cb, row0, grp, carry):
        s, sq = carry
        acc = taps_pass(glu_p, cb, row0, lambda o: o, grp)
        for g in range(grp):
            kept = jnp.where(live_of(row0 + 8 * g, 8, 128), acc[g], 0.0)
            conv_v[cb, pl.ds(row0 + 8 * g, 8), :] = kept
            s = s + kept
            sq = sq + kept * kept
        return s, sq

    EDGE, INNER = 8, 16

    def conv_inner(cb):
        s = sq = jnp.zeros((8, 128), F32)
        for i in range((ROWS - 128) // 128):
            s, sq = conv_rows(cb, 64 + i * 128, INNER, (s, sq))
        stat_v[cb, 0] = s
        stat_v[cb, 1] = sq

    pl.loop(0, 2)(conv_inner)
    pl.semaphore_wait(barrier, NTM + NDP - 2)
    halo_g[0]()
    pl.loop(2, CB)(conv_inner)
    halo_g[1]()

    @pl.loop(0, CB)
    def _(cb):
        s, sq = stat_v[cb, 0], stat_v[cb, 1]
        for row0 in (0, ROWS - 64):
            s, sq = conv_rows(cb, row0, EDGE, (s, sq))
        red[0, pl.ds(cb, 1), :] = jnp.sum(s, axis=0, keepdims=True)
        red[1, pl.ds(cb, 1), :] = jnp.sum(sq, axis=0, keepdims=True)

    def spread(axis, count, src_of, dst, ss, rs):
        me = tm if axis == "tm" else dp

        def copy(d, slot):
            peer = (me + d) % count
            dev = (dp, peer) if axis == "tm" else (peer, tm)
            return rcopy(src_of(peer), dst.at[slot], ss.at[d], rs.at[slot], dev)

        def start():
            for d in range(1, count):
                copy(d, me).start()

        def recv():
            for d in range(1, count):
                copy(d, (me + d) % count).wait_recv()

        def sent():
            for d in range(1, count):
                copy(d, me).wait_send()

        return start, recv, sent

    def total(ref, count):
        acc = ref[0].astype(F32)
        for i in range(1, count):
            acc = acc + ref[i].astype(F32)
        return acc

    def all_sum(n):
        one = spread("tm", NTM, lambda p: red_in.at[n], red_rx1.at[n], ar1_s.at[n], ar1_r.at[n])
        two = spread("dp", NDP, lambda p: red_mid.at[n], red_rx2.at[n], ar2_s.at[n], ar2_r.at[n])

        def begin():
            v = red[...]
            red_in[n] = v
            red_rx1[n, tm] = v
            one[0]()

        def middle():
            one[1]()
            v = total(red_rx1.at[n], NTM)
            red_mid[n] = v
            red_rx2[n, dp] = v
            two[0]()

        def end():
            two[1]()
            return total(red_rx2.at[n], NDP)

        def sent():
            one[2]()
            two[2]()

        return begin, middle, end, sent

    ar_a, ar_b = all_sum(0), all_sum(1)
    ar_a[0]()

    loads[1].wait()
    loads[2].wait()

    @pl.loop(0, 4)
    def _(j):
        c0 = pl.multiple_of(j * 256, 256)
        ds = dot_nt(cot[...], w_out[pl.ds(c0, 256), :])
        for h in range(2):
            dsh_v[2 * j + h] = ds[:, h * 128 : h * 128 + 128]

    def tap_sums(dst, grad, first_blocks, between):
        grp = 16

        @pl.loop(0, CB)
        def _(cb):
            pl.when(cb == first_blocks)(between)

            def step(i, accs):
                row0 = pl.multiple_of(i * (8 * grp), 8 * grp)
                accs = list(accs)
                ds = [grad[cb, pl.ds(row0 + 8 * g, 8), :] for g in range(grp)]
                for r in range(8):
                    xs = [glu_p[cb, pl.ds(row0 + (8 * n + r), 8), :] for n in range(grp + 3)]
                    for q in range(4):
                        o = 8 * q + r
                        if o == 0:
                            continue
                        for g in range(grp):
                            accs[o - 1] = accs[o - 1] + xs[g + q] * ds[g]
                return tuple(accs)

            zero = jnp.zeros((8, 128), F32)
            accs = lax.fori_loop(0, ROWS // (8 * grp), step, (zero,) * TAPS)
            for k in range(TAPS):
                dst[k + 1, pl.ds(cb, 1), :] = jnp.sum(accs[k], axis=0, keepdims=True)

    def window(rows_of):
        count = jnp.clip(limit, 0, ROWS)
        row, tap = rows_of
        return ((row >= tap) & (row < count + tap)).astype(F32).astype(BF16)

    def live_sums():
        def grid(n):
            return [lax.broadcasted_iota(jnp.int32, (32, n), d) for d in (1, 0)]

        row, tap = grid(ROWS)
        inner = window((row + PAD, tap))
        row, tap = grid(2 * PAD)
        outer = window((jnp.where(row < PAD, row, row + ROWS), tap))
        for cb in range(CB):
            ends = jnp.concatenate(
                [glu_p[cb, 0:PAD, :], glu_p[cb, PAD + ROWS : PROWS, :]], axis=0
            )
            gk2[:, cb, :] = dot_nn(inner, glu_p[cb, PAD : PAD + ROWS, :].astype(BF16)) + dot_nn(
                outer, ends.astype(BF16)
            )

    tap_sums(gk3, conv_v, 1, ar_a[1])
    sums = ar_a[2]()
    mean = sums[0] * (1.0 / COUNT)
    variance = sums[1] * (1.0 / COUNT) - mean * mean
    inv_std = lax.rsqrt(variance + 1e-05)
    vec[0] = mean
    vec[1] = inv_std
    vec[2] = gain_ref[...]
    vec[3] = bias_ref[...]

    @pl.loop(0, CB)
    def _(cb):
        mean_r = vec[0, pl.ds(cb, 1), :]
        inv_r = vec[1, pl.ds(cb, 1), :]
        gain_r = vec[2, pl.ds(cb, 1), :]
        bias_r = vec[3, pl.ds(cb, 1), :]

        def step(i, carry):
            sg, sb = carry
            n = 256
            row0 = pl.multiple_of(i * n, n)
            live = live_of(row0, n, 128)
            normed = (conv_v[cb, pl.ds(row0, n), :] - mean_r) * inv_r
            shifted = gain_r * normed + bias_r
            act = sigmoid(shifted)
            sw_v[cb, pl.ds(row0, n), :] = jnp.where(live, shifted * act, 0.0).astype(BF16)
            slope = act * (1.0 + shifted * (1.0 - act))
            dsh = jnp.where(live, dsh_v[cb, pl.ds(row0, n), :] * slope, 0.0)
            dsh_v[cb, pl.ds(row0, n), :] = dsh
            conv_v[cb, pl.ds(row0, n), :] = normed
            prod = dsh * normed
            for g in range(n // 8):
                sg = sg + prod[8 * g : 8 * g + 8]
                sb = sb + dsh[8 * g : 8 * g + 8]
            return sg, sb

        zero = jnp.zeros((8, 128), F32)
        sg, sb = lax.fori_loop(0, ROWS // 256, step, (zero, zero))
        red[0, pl.ds(cb, 1), :] = jnp.sum(sg, axis=0, keepdims=True)
        red[1, pl.ds(cb, 1), :] = jnp.sum(sb, axis=0, keepdims=True)

    ar_b[0]()

    def buf(name, b):
        whole, pairs, singles = rs_bufs[name]
        return whole if b == 0 else pairs.at[b - 1] if b < 4 else singles.at[b - 4]

    rs_bufs = {
        "wl": (wl_a, wl_b, wl_c), "crx": (crx_a, crx_b, crx_c), "cs": (cs_a, cs_b, cs_c),
        "r1": (r1_a, r1_b, r1_c), "s1": (s1_a, s1_b, s1_c), "r2": (r2_a, r2_b, r2_c),
        "s2": (s2_a, s2_b, s2_c), "r3": (r3_a, r3_b, r3_c),
    }

    def put_terms(dst, rows, cols, first, second):
        n, w = first.shape[0] // 16, first.shape[1]
        both = jnp.concatenate([first.reshape(n, 2, 8, w), second.reshape(n, 2, 8, w)], axis=2)
        dst[pl.ds(n * rows, n), :, :, cols] = both.astype(BF16)

    def rs_core(b):
        return rcopy(
            buf("wl", b).at[:, 1 - core], buf("crx", b), rs_s.at[b, 0], rs_r.at[b, 0],
            (dp, tm + 1 - 2 * core),
        )

    def part_of(ref, dims, axis, p):
        at = dims.index(axis)
        return ref.at[tuple(slice(None) for _ in range(at)) + (p,)]

    def rs_copies(b, stage):
        dims = ("z", "x", "y")
        if b == 0:
            src, dst = (("cs", "r1"), ("s1", "r2"), ("s2", "r3"))[stage]
            dims = tuple(a for a in dims if a not in ORDER[:stage])
            axis = ORDER[stage]
        else:
            src, dst = (("cs", "r1"), ("s1", "r2"))[stage]
            axis = ("y", "dp")[stage]
        src, dst = buf(src, b), buf(dst, b)
        copies = []
        if axis == "dp":
            for d in range(1, NDP):
                p = (dp + d) % NDP
                copies.append(
                    rcopy(
                        src.at[p // 4, p % 4], dst.at[d - 1],
                        rs_s.at[b, 3 + d], rs_r.at[b, 3 + d], (p, tm),
                    )
                )
            return copies, src.at[z, x], dst
        for d in range(1, 4):
            p = (pos[axis] + d) % 4
            copies.append(
                rcopy(
                    part_of(src, dims, axis, p), dst.at[d - 1],
                    rs_s.at[b, 3 * stage + d], rs_r.at[b, 3 * stage + d], at_axis(axis, p),
                )
            )
        return copies, part_of(src, dims, axis, pos[axis]), dst

    def stages(b):
        return 3 if b == 0 else 2

    def rs_one(b):
        rs_core(b).wait_recv()

        @pl.loop(0, 4)
        def _(i):
            rows = pl.ds(i * 16, 16)
            both = buf("wl", b)[rows, core].astype(F32) + buf("crx", b)[rows].astype(F32)
            buf("cs", b)[i] = both.astype(BF16).reshape(4, 4, 16, both.shape[-1])

        for c in rs_copies(b, 0)[0]:
            c.start()

    def rs_next(b, stage):
        copies, own, got = rs_copies(b, stage)
        for c in copies:
            c.wait_recv()
        acc = own[...].astype(F32)
        for d in range(len(copies)):
            acc = acc + got[d].astype(F32)
        if stage < stages(b) - 1:
            buf(("s1", "s2")[stage], b)[...] = acc.astype(BF16)
            for c in rs_copies(b, stage + 1)[0]:
                c.start()
        else:
            acc = acc * SCALE
            if b == 0:
                gwo_ref[:, 0:512] = acc[0:8]
                gwo_ref[:, 512:1024] = acc[8:16]
            else:
                c0, w = (256 * (b - 1), 256) if b < 4 else (128 * (b + 2), 128)
                gwi_ref[:, c0 : c0 + w] = acc[0:8]
                gwi_ref[:, CH + c0 : CH + c0 + w] = acc[8:16]

    for half in range(2):
        cols = slice(256 * half, 256 * half + 256)
        for i in range(2):
            rows = jnp.concatenate([sw_v[4 * i + e] for e in range(4)], axis=1)
            put_terms(
                wl_a, i, cols,
                dot_tn(rows, cot[:, 256 * half : 256 * half + 256]),
                dot_tn(rows, cot[:, 512 + 256 * half : 512 + 256 * half + 256]),
            )

    rs_core(0).start()
    tap_sums(gk1, dsh_v, 2, ar_b[1])
    live_sums()
    rs_one(0)

    grads = ar_b[2]()
    gg_ref[...] = grads[0] * SCALE
    gb_ref[...] = grads[1] * SCALE
    vec[4] = gain_ref[...] * vec[1]
    vec[5] = grads[1] * (1.0 / COUNT)
    vec[6] = grads[0] * (1.0 / COUNT)

    def dconv_rows(parts):
        @pl.loop(0, CB)
        def _(cb):
            factor = vec[4, pl.ds(cb, 1), :]
            shift = vec[5, pl.ds(cb, 1), :]
            tilt = vec[6, pl.ds(cb, 1), :]
            for row0, n in parts:
                rows = pl.ds(row0, n)
                inner = dsh_v[cb, rows, :] - shift - conv_v[cb, rows, :] * tilt
                dcv = jnp.where(live_of(row0, n, 128), factor * inner, 0.0)
                dcv_p[cb, pl.ds(PAD + row0, n), :] = dcv.astype(BF16).astype(F32)

    dconv_rows(((0, PAD), (ROWS - PAD, PAD)))
    halo_d[0]()

    mean, inv_std = vec[0], vec[1]

    def tap_row(k):
        if k == TAPS:
            return jnp.zeros((8, 128), F32)
        tilted = inv_std * (gk3[k + 1] - mean * gk2[k + 1])
        return vec[4] * (gk1[k + 1] - vec[5] * gk2[k + 1] - vec[6] * tilted)

    for k in range(0, 32, 2):
        gkl[k // 2] = jnp.concatenate([tap_row(k), tap_row(k + 1)], axis=0).astype(BF16)

    kt1 = spread("tm", NTM, lambda p: gkl.at[pl.ds(2 * p, 2)], kr1, k1_s, k1_r)
    kt2 = spread("dp", NDP, lambda p: ks1, kr2, k2_s, k2_r)
    kt3 = spread("tm", NTM, lambda p: ks2, kfull, k3_s, k3_r)
    def back_rows(cb, row0, grp):
        acc = taps_pass(dcv_p, cb, row0, lambda o: 32 - o, grp)
        for g in range(0, grp, 2):
            dl, dg = [], []
            for e in (g, g + 1):
                rows = pl.ds(row0 + 8 * e, 8)
                dglu = jnp.where(live_of(row0 + 8 * e, 8, 128), acc[e], 0.0)
                sig = sig_v[cb, rows, :]
                half = dglu * sig
                dl.append(half)
                dg.append(half * lin_v[cb, rows, :] * (1.0 - sig))
            rows = pl.ds(row0 + 8 * g, 16)
            dpre_v[cb, rows, :] = jnp.concatenate(dl, axis=0).astype(BF16)
            dpre_v[CB + cb, rows, :] = jnp.concatenate(dg, axis=0).astype(BF16)

    def back_inner(cb):
        for i in range((ROWS - 128) // 128):
            back_rows(cb, 64 + 128 * i, INNER)

    def back_edges(cb):
        for row0 in (0, ROWS - 64):
            back_rows(cb, row0, EDGE)

    def back_all(cb):
        for i in range(GROUPS):
            back_rows(cb, 8 * GRP * i, GRP)

    def pair_terms(j):
        first = jnp.concatenate([dpre_v[2 * j], dpre_v[2 * j + 1]], axis=1)
        second = jnp.concatenate([dpre_v[CB + 2 * j], dpre_v[CB + 2 * j + 1]], axis=1)

        @pl.loop(0, 2)
        def _(i):
            rows = feats[:, pl.ds(pl.multiple_of(512 * i, 512), 512)]
            put_terms(buf("wl", 1 + j), i, slice(None), dot_tn(rows, first), dot_tn(rows, second))

        rs_core(1 + j).start()

    def single_terms(b):
        cb = b + 2
        both = jnp.concatenate([dpre_v[cb], dpre_v[CB + cb]], axis=1)

        @pl.loop(0, 2)
        def _(i):
            rows = feats[:, pl.ds(pl.multiple_of(512 * i, 512), 512)]
            part = dot_tn(rows, both)
            put_terms(buf("wl", b), i, slice(None), part[:, 0:128], part[:, 128:256])

        rs_core(b).start()

    def kt_sum(n):
        if n == 0:
            kr1[tm] = gkl[pl.ds(2 * tm, 2)]
            kt1[0]()
        elif n == 1:
            kt1[1]()
            v = total(kr1, NTM).astype(BF16)
            ks1[...] = v
            kr2[dp] = v
            kt2[0]()
        elif n == 2:
            kt2[1]()
            v = total(kr2, NDP)
            ks2[...] = v
            kfull[tm] = v
            kt3[0]()
        else:
            kt3[1]()
            for cb in range(CB):
                for k in range(TAPS):
                    at = 8 * (k % 2) + cb
                    row = kfull[k // 4, k % 4 // 2, at : at + 1, :]
                    gk_ref[k : k + 1, 128 * cb : 128 * cb + 128] = row * SCALE

    def frame_cols(j):
        rows = jnp.concatenate([dpre_v[c] for c in range(2 * CB)], axis=1)
        part = dot_nt(rows, w_in[256 * j : 256 * j + 256, :])
        out_v[1, :, 256 * j : 256 * j + 256] = part.astype(BF16)

    def out_cols(j):
        rows = jnp.concatenate([sw_v[cb] for cb in range(CB)], axis=1)
        part = dot_nn(rows, w_out[:, 256 * j : 256 * j + 256])
        out_v[0, :, 256 * j : 256 * j + 256] = part.astype(BF16)

    kt_sum(0)
    dconv_rows(((PAD, 384), (PAD + 384, 352)))
    pl.loop(0, 2)(back_inner)
    halo_d[1]()
    pl.loop(0, 2)(back_edges)
    pair_terms(0)
    kt_sum(1)
    pl.loop(2, 4)(back_all)
    pair_terms(1)
    rs_one(1)
    pl.loop(4, 6)(back_all)
    pair_terms(2)
    rs_one(2)
    kt_sum(2)
    rs_next(0, 0)
    pl.loop(6, 7)(back_all)
    single_terms(4)
    rs_one(3)
    pl.loop(7, 8)(back_all)
    single_terms(5)
    rs_one(4)

    frame_cols(0)
    rs_one(5)
    rs_next(1, 0)
    frame_cols(1)
    frame_cols(2)
    rs_next(0, 1)
    frame_cols(3)
    gf_copy = pltpu.make_async_copy(out_v.at[1], gf_h, out_sem.at[1])
    gf_copy.start()
    rs_next(2, 0)
    out_cols(0)
    out_cols(1)
    rs_next(3, 0)
    out_cols(2)
    out_cols(3)
    out_copy = pltpu.make_async_copy(out_v.at[0], out_h, out_sem.at[0])
    out_copy.start()
    rs_next(4, 0)
    rs_next(5, 0)
    kt_sum(3)
    rs_next(0, 2)
    rs_next(1, 1)
    rs_next(2, 1)
    rs_next(3, 1)
    rs_next(4, 1)
    rs_next(5, 1)

    for t in (halo_g, halo_d, kt1, kt2, kt3):
        t[2]()
    ar_a[3]()
    ar_b[3]()
    for b in range(NB):
        rs_core(b).wait_send()
        for stage in range(stages(b)):
            for c in rs_copies(b, stage)[0]:
                c.wait_send()
    out_copy.wait()
    gf_copy.wait()


SCALE = 1.0 / math.sqrt(16 * 6144)


def rs_scratch(lead, width):
    shapes = [(64, 2), (64,), (4, 4, 4), (3, 4, 4), (4, 4), (3, 4), (4,), (3,)]
    if lead:
        shapes[5:] = [(15,), (1,), (1,)]
    return [pltpu.VMEM((*lead, *s, 16, width), BF16) for s in shapes]


PIECES = ((0, 4), (1, 4), (2, 1), (3, 1), (4, 1), (5, 1), (6, 1))


def hand_over(*refs):
    srcs, dsts, held, sems = refs[0:7], refs[7:14], refs[14:21], refs[21]
    steps = []
    for i, parts in PIECES:
        rows = srcs[i].shape[0] // parts
        for p in range(parts):
            at = (pl.ds(p * rows, rows),)
            n = len(steps)
            steps.append((
                pltpu.make_async_copy(srcs[i].at[at], held[i].at[at], sems.at[n, 0]),
                pltpu.make_async_copy(held[i].at[at], dsts[i].at[at], sems.at[n, 1]),
            ))
    for come, _ in steps:
        come.start()
    for come, go in steps:
        come.wait()
        go.start()
    for _, go in steps:
        go.wait()


def local(frames, lengths, w_in, w_dw, bn_gain, bn_bias, w_out, cotangent):
    hbm = pl.BlockSpec(memory_space=pl.ANY)
    vmem = pl.BlockSpec(memory_space=pltpu.VMEM)
    smem = pl.BlockSpec(memory_space=pltpu.SMEM)
    dma = pltpu.SemaphoreType.DMA
    outs = pl.pallas_call(
        kernel,
        out_shape=(
            jax.ShapeDtypeStruct((ROWS, CH), BF16),
            jax.ShapeDtypeStruct((ROWS, CH), BF16),
            jax.ShapeDtypeStruct((8, 2 * CH), F32),
            jax.ShapeDtypeStruct((8, CH), F32),
            jax.ShapeDtypeStruct((TAPS, CH), F32),
            jax.ShapeDtypeStruct((8, 128), F32),
            jax.ShapeDtypeStruct((8, 128), F32),
        ),
        in_specs=[smem, hbm, hbm, vmem, vmem, vmem, hbm, hbm],
        out_specs=(hbm, hbm, vmem, vmem, vmem, vmem, vmem),
        scratch_shapes=[
            pltpu.VMEM((ROWS, CH), BF16),
            pltpu.VMEM((CH, 2 * CH), BF16),
            pltpu.VMEM((CH, CH), BF16),
            pltpu.VMEM((ROWS, CH), BF16),
            pltpu.VMEM((CB, 2, 8, 128), F32),
            pltpu.VMEM((CB, ROWS, 128), F32),
            pltpu.VMEM((CB, ROWS, 128), F32),
            pltpu.VMEM((CB, PROWS, 128), F32),
            pltpu.VMEM((CB, PROWS, 128), F32),
            pltpu.VMEM((CB, ROWS, 128), F32),
            pltpu.VMEM((CB, ROWS, 128), F32),
            pltpu.VMEM((CB, ROWS, 128), BF16),
            pltpu.VMEM((2 * CB, ROWS, 128), BF16),
            pltpu.VMEM((2, ROWS, CH), BF16),
            pltpu.VMEM((CB, 32, 8, 128), F32),
            pltpu.VMEM((8, 8, 128), F32),
            pltpu.VMEM((2, 8, 128), F32),
            pltpu.VMEM((2, 2, 8, 128), F32),
            pltpu.VMEM((2, 2, 8, 128), F32),
            pltpu.VMEM((2, NTM, 2, 8, 128), F32),
            pltpu.VMEM((2, NDP, 2, 8, 128), F32),
            pltpu.VMEM((16, 16, 128), BF16),
            pltpu.VMEM((32, 8, 128), F32),
            pltpu.VMEM((32, 8, 128), F32),
            pltpu.VMEM((32, 8, 128), F32),
            pltpu.VMEM((NTM, 2, 16, 128), BF16),
            pltpu.VMEM((2, 16, 128), BF16),
            pltpu.VMEM((NDP, 2, 16, 128), BF16),
            pltpu.VMEM((2, 16, 128), F32),
            pltpu.VMEM((NTM, 2, 16, 128), F32),
            *rs_scratch((), 512),
            *rs_scratch((3,), 256),
            *rs_scratch((2,), 128),
            dma((3,)),
            dma((4, 2)),
            dma((2,)),
            dma((4,)),
            dma((4,)),
            dma((2, NTM)),
            dma((2, NTM)),
            dma((2, NDP)),
            dma((2, NDP)),
            dma((NTM,)),
            dma((NTM,)),
            dma((NDP,)),
            dma((NDP,)),
            dma((NTM,)),
            dma((NTM,)),
            dma((NB, 19)),
            dma((NB, 19)),
        ],
        compiler_params=pltpu.CompilerParams(
            collective_id=0, has_side_effects=True, vmem_limit_bytes=62 << 20
        ),
        name="conformer_conv",
    )(
        lengths, frames[0], w_in, w_dw, bn_gain.reshape(8, 128), bn_bias.reshape(8, 128),
        w_out, cotangent[0],
    )
    out, gf, gwi, gwo, gk, gg, gb = pl.pallas_call(
        hand_over,
        out_shape=tuple(jax.ShapeDtypeStruct(o.shape, o.dtype) for o in outs),
        in_specs=[hbm] * 7,
        out_specs=(hbm,) * 7,
        scratch_shapes=[pltpu.VMEM(o.shape, o.dtype) for o in outs] + [dma((13, 2))],
        name="hand_over",
    )(*outs)
    return (out[None], gf[None], gwi, gwo, gk, gg.reshape(CH), gb.reshape(CH))


def solution(mesh):
    placed = (P("dp", "tm", None), P("dp"), P(), P(), P(), P(), P(), P("dp", "tm", None))
    return jax.shard_map(
        local,
        mesh=mesh,
        in_specs=placed,
        out_specs=(
            P("dp", "tm", None),
            P("dp", "tm", None),
            P(("dp", "tm"), None),
            P(("dp", "tm"), None),
            P(),
            P(),
            P(),
        ),
        check_vma=False,
    )
```

```python
import math

import jax
import jax.numpy as jnp
from jax import lax
from jax.experimental import pallas as pl
from jax.experimental.pallas import tpu as pltpu
from jax.sharding import PartitionSpec as P

MESH_ID = pl.DeviceIdType.MESH
F32 = jnp.float32
BF16 = jnp.bfloat16

ROWS = 768
CH = 1024
CB = 8
PAD = 16
PROWS = ROWS + 2 * PAD
TAPS = 31
COUNT = 58982.0
NDP, NTM = 16, 8
GRP = 12
GROUPS = ROWS // (8 * GRP)
NB = 5
ORDER = ("z", "x", "y")


def sigmoid(x):
    return 0.5 * jnp.tanh(0.5 * x) + 0.5


def dot_nn(a, b):
    return lax.dot_general(a, b, (((1,), (0,)), ((), ())), preferred_element_type=F32)


def dot_tn(a, b):
    return lax.dot_general(a, b, (((0,), (0,)), ((), ())), preferred_element_type=F32)


def dot_nt(a, b):
    return lax.dot_general(a, b, (((1,), (1,)), ((), ())), preferred_element_type=F32)


def kernel(
    len_ref, frames_h, w_in_h, w_dw, gain_ref, bias_ref, w_out_h, cot_h,
    out_h, gf_h, gwi_ref, gwo_ref, gk_ref, gg_ref, gb_ref,
    feats, w_in, w_out, cot, stat_v, lin_v, sig_v, glu_p, dcv_p, conv_v, dsh_v,
    sw_v, dpre_v, out_v, wb, vec,
    red, red_in, red_mid, red_rx1, red_rx2,
    gkl, gk1, gk2, gk3, kr1, ks1, kr2, ks2, kfull,
    wl_a, crx_a, cs_a, r1_a, s1_a, r2_a, s2_a, r3_a,
    wl_b, crx_b, cs_b, r1_b, s1_b, r2_b,
    wl_c, crx_c, cs_c, r1_c, s1_c, r2_c,
    in_sem, w_sem, out_sem, halo_s, halo_r, ar1_s, ar1_r, ar2_s, ar2_r,
    k1_s, k1_r, k2_s, k2_r, k3_s, k3_r, rs_s, rs_r,
):
    dp = lax.axis_index("dp")
    tm = lax.axis_index("tm")
    z, x = dp // 4, dp % 4
    y, core = tm // 2, tm % 2
    pos = {"z": z, "x": x, "y": y}

    def at_axis(axis, p):
        if axis == "z":
            return (p * 4 + x, tm)
        if axis == "x":
            return (z * 4 + p, tm)
        return (dp, p * 2 + core)

    def rcopy(src, dst, ss, rs, dev):
        return pltpu.make_async_remote_copy(
            src_ref=src, dst_ref=dst, send_sem=ss, recv_sem=rs,
            device_id=dev, device_id_type=MESH_ID,
        )

    def w_in_load(j, half):
        cols = pl.ds(half * CH + j * 256, 256)
        return pltpu.make_async_copy(w_in_h.at[:, cols], w_in.at[:, cols], w_sem.at[j, half])

    loads = [
        pltpu.make_async_copy(frames_h, feats, in_sem.at[0]),
        pltpu.make_async_copy(cot_h, cot, in_sem.at[1]),
        pltpu.make_async_copy(w_out_h, w_out, in_sem.at[2]),
    ]
    loads[0].start()
    for j in range(4):
        for half in range(2):
            w_in_load(j, half).start()
    loads[1].start()
    loads[2].start()
    barrier = pltpu.get_barrier_semaphore()
    for d in range(1, NTM):
        pl.semaphore_signal(barrier, inc=1, device_id=(dp, (tm + d) % NTM), device_id_type=MESH_ID)
    for d in range(1, NDP):
        pl.semaphore_signal(barrier, inc=1, device_id=((dp + d) % NDP, tm), device_id_type=MESH_ID)

    limit = len_ref[0] - tm * ROWS

    def live_of(row0, rows, cols):
        t = lax.broadcasted_iota(jnp.int32, (rows, cols), 0) + row0
        return t < limit

    @pl.loop(0, TAPS)
    def _(k):
        row = w_dw[pl.ds(k, 1), :]
        for cb in range(CB):
            wb[cb, k + 1] = jnp.broadcast_to(row[:, cb * 128 : cb * 128 + 128], (8, 128))

    for ref in (glu_p, dcv_p):
        @pl.when(tm == 0)
        def _():
            ref[:, 0:PAD, :] = jnp.zeros((CB, PAD, 128), F32)

        @pl.when(tm == NTM - 1)
        def _():
            ref[:, PAD + ROWS : PROWS, :] = jnp.zeros((CB, PAD, 128), F32)

    loads[0].wait()

    @pl.loop(0, 4)
    def _(j):
        c0 = pl.multiple_of(j * 256, 256)
        w_in_load(j, 0).wait()
        w_in_load(j, 1).wait()
        rows = feats[...]
        lin = dot_nn(rows, w_in[:, pl.ds(c0, 256)])
        sig = sigmoid(dot_nn(rows, w_in[:, pl.ds(CH + c0, 256)]))
        glu = jnp.where(live_of(0, ROWS, 256), lin * sig, 0.0).astype(BF16).astype(F32)
        for h in range(2):
            cols = slice(h * 128, h * 128 + 128)
            lin_v[2 * j + h] = lin[:, cols]
            sig_v[2 * j + h] = sig[:, cols]
            glu_p[2 * j + h, pl.ds(PAD, ROWS), :] = glu[:, cols]

    def halo(ref, n):
        to_left = rcopy(
            ref.at[:, pl.ds(PAD, PAD), :], ref.at[:, pl.ds(PAD + ROWS, PAD), :],
            halo_s.at[n], halo_r.at[n], (dp, (tm + NTM - 1) % NTM),
        )
        to_right = rcopy(
            ref.at[:, pl.ds(ROWS, PAD), :], ref.at[:, pl.ds(0, PAD), :],
            halo_s.at[n + 1], halo_r.at[n + 1], (dp, (tm + 1) % NTM),
        )

        def start():
            pl.when(tm > 0)(to_left.start)
            pl.when(tm < NTM - 1)(to_right.start)

        def recv():
            pl.when(tm < NTM - 1)(to_left.wait_recv)
            pl.when(tm > 0)(to_right.wait_recv)

        def sent():
            pl.when(tm > 0)(to_left.wait_send)
            pl.when(tm < NTM - 1)(to_right.wait_send)

        return start, recv, sent

    halo_g, halo_d = halo(glu_p, 0), halo(dcv_p, 2)
    def taps_pass(src, cb, row0, tap_of, grp):
        acc = [None] * grp
        for r in range(8):
            xs = [src[cb, pl.ds(row0 + (8 * n + r), 8), :] for n in range(grp + 3)]
            for q in range(4):
                o = 8 * q + r
                if o == 0:
                    continue
                w = wb[cb, tap_of(o)]
                for g in range(grp):
                    term = w * xs[g + q]
                    acc[g] = term if acc[g] is None else acc[g] + term
        return acc

    def conv_rows(cb, row0, grp, carry):
        s, sq = carry
        acc = taps_pass(glu_p, cb, row0, lambda o: o, grp)
        for g in range(grp):
            kept = jnp.where(live_of(row0 + 8 * g, 8, 128), acc[g], 0.0)
            conv_v[cb, pl.ds(row0 + 8 * g, 8), :] = kept
            s = s + kept
            sq = sq + kept * kept
        return s, sq

    EDGE, INNER = 8, 16

    def conv_inner(cb):
        def step(i, carry):
            return conv_rows(cb, pl.multiple_of(64 + i * 128, 64), INNER, carry)

        zero = jnp.zeros((8, 128), F32)
        s, sq = lax.fori_loop(0, (ROWS - 128) // 128, step, (zero, zero))
        stat_v[cb, 0] = s
        stat_v[cb, 1] = sq

    def meet():
        pl.semaphore_wait(barrier, NTM + NDP - 2)
        halo_g[0]()

    @pl.loop(0, CB)
    def _(cb):
        pl.when(cb == 2)(meet)
        conv_inner(cb)

    halo_g[1]()

    @pl.loop(0, CB)
    def _(cb):
        def step(i, carry):
            return conv_rows(cb, pl.multiple_of(i * (ROWS - 64), 64), EDGE, carry)

        s, sq = lax.fori_loop(0, 2, step, (stat_v[cb, 0], stat_v[cb, 1]))
        red[0, pl.ds(cb, 1), :] = jnp.sum(s, axis=0, keepdims=True)
        red[1, pl.ds(cb, 1), :] = jnp.sum(sq, axis=0, keepdims=True)

    def spread(axis, count, src_of, dst, ss, rs):
        me = tm if axis == "tm" else dp

        def copy(d, slot):
            peer = (me + d) % count
            dev = (dp, peer) if axis == "tm" else (peer, tm)
            return rcopy(src_of(peer), dst.at[slot], ss.at[d], rs.at[slot], dev)

        def start():
            for d in range(1, count):
                copy(d, me).start()

        def recv():
            for d in range(1, count):
                copy(d, (me + d) % count).wait_recv()

        def sent():
            for d in range(1, count):
                copy(d, me).wait_send()

        return start, recv, sent

    def total(ref, count):
        acc = ref[0].astype(F32)
        for i in range(1, count):
            acc = acc + ref[i].astype(F32)
        return acc

    def all_sum(n):
        one = spread("tm", NTM, lambda p: red_in.at[n], red_rx1.at[n], ar1_s.at[n], ar1_r.at[n])
        two = spread("dp", NDP, lambda p: red_mid.at[n], red_rx2.at[n], ar2_s.at[n], ar2_r.at[n])

        def begin():
            v = red[...]
            red_in[n] = v
            red_rx1[n, tm] = v
            one[0]()

        def middle():
            one[1]()
            v = total(red_rx1.at[n], NTM)
            red_mid[n] = v
            red_rx2[n, dp] = v
            two[0]()

        def end():
            two[1]()
            return total(red_rx2.at[n], NDP)

        def sent():
            one[2]()
            two[2]()

        return begin, middle, end, sent

    ar_a, ar_b = all_sum(0), all_sum(1)
    ar_a[0]()

    loads[1].wait()
    loads[2].wait()

    @pl.loop(0, 4)
    def _(j):
        c0 = pl.multiple_of(j * 256, 256)
        ds = dot_nt(cot[...], w_out[pl.ds(c0, 256), :])
        for h in range(2):
            dsh_v[2 * j + h] = ds[:, h * 128 : h * 128 + 128]

    def tap_sums(dst, grad, first_blocks, between):
        grp = 16

        @pl.loop(0, CB)
        def _(cb):
            pl.when(cb == first_blocks)(between)

            def step(i, accs):
                row0 = pl.multiple_of(i * (8 * grp), 8 * grp)
                accs = list(accs)
                ds = [grad[cb, pl.ds(row0 + 8 * g, 8), :] for g in range(grp)]
                for r in range(8):
                    xs = [glu_p[cb, pl.ds(row0 + (8 * n + r), 8), :] for n in range(grp + 3)]
                    for q in range(4):
                        o = 8 * q + r
                        if o == 0:
                            continue
                        for g in range(grp):
                            accs[o - 1] = accs[o - 1] + xs[g + q] * ds[g]
                return tuple(accs)

            zero = jnp.zeros((8, 128), F32)
            accs = lax.fori_loop(0, ROWS // (8 * grp), step, (zero,) * TAPS)
            for k in range(TAPS):
                dst[k + 1, pl.ds(cb, 1), :] = jnp.sum(accs[k], axis=0, keepdims=True)

    def window(rows_of):
        count = jnp.clip(limit, 0, ROWS)
        row, tap = rows_of
        return ((row >= tap) & (row < count + tap)).astype(F32).astype(BF16)

    def live_sums():
        def grid(n):
            return [lax.broadcasted_iota(jnp.int32, (32, n), d) for d in (1, 0)]

        row, tap = grid(ROWS)
        inner = window((row + PAD, tap))
        row, tap = grid(2 * PAD)
        outer = window((jnp.where(row < PAD, row, row + ROWS), tap))
        for cb in range(CB):
            ends = jnp.concatenate(
                [glu_p[cb, 0:PAD, :], glu_p[cb, PAD + ROWS : PROWS, :]], axis=0
            )
            gk2[:, cb, :] = dot_nn(inner, glu_p[cb, PAD : PAD + ROWS, :].astype(BF16)) + dot_nn(
                outer, ends.astype(BF16)
            )

    tap_sums(gk3, conv_v, 1, ar_a[1])
    sums = ar_a[2]()
    mean = sums[0] * (1.0 / COUNT)
    variance = sums[1] * (1.0 / COUNT) - mean * mean
    inv_std = lax.rsqrt(variance + 1e-05)
    vec[0] = mean
    vec[1] = inv_std
    vec[2] = gain_ref[...]
    vec[3] = bias_ref[...]

    @pl.loop(0, CB)
    def _(cb):
        mean_r = vec[0, pl.ds(cb, 1), :]
        inv_r = vec[1, pl.ds(cb, 1), :]
        gain_r = vec[2, pl.ds(cb, 1), :]
        bias_r = vec[3, pl.ds(cb, 1), :]

        def step(i, carry):
            sg, sb = carry
            n = 256
            row0 = pl.multiple_of(i * n, n)
            live = live_of(row0, n, 128)
            normed = (conv_v[cb, pl.ds(row0, n), :] - mean_r) * inv_r
            shifted = gain_r * normed + bias_r
            act = sigmoid(shifted)
            sw_v[cb, pl.ds(row0, n), :] = jnp.where(live, shifted * act, 0.0).astype(BF16)
            slope = act * (1.0 + shifted * (1.0 - act))
            dsh = jnp.where(live, dsh_v[cb, pl.ds(row0, n), :] * slope, 0.0)
            dsh_v[cb, pl.ds(row0, n), :] = dsh
            conv_v[cb, pl.ds(row0, n), :] = normed
            prod = dsh * normed
            for g in range(n // 8):
                sg = sg + prod[8 * g : 8 * g + 8]
                sb = sb + dsh[8 * g : 8 * g + 8]
            return sg, sb

        zero = jnp.zeros((8, 128), F32)
        sg, sb = lax.fori_loop(0, ROWS // 256, step, (zero, zero))
        red[0, pl.ds(cb, 1), :] = jnp.sum(sg, axis=0, keepdims=True)
        red[1, pl.ds(cb, 1), :] = jnp.sum(sb, axis=0, keepdims=True)

    ar_b[0]()

    A = ("a", None)
    rs_bufs = {
        "a": dict(wl=wl_a, crx=crx_a, cs=cs_a, r1=r1_a, s1=s1_a, r2=r2_a, s2=s2_a, r3=r3_a),
        "y": dict(wl=wl_b, crx=crx_b, cs=cs_b, r1=r1_b, s1=s1_b, r2=r2_b),
        "dp": dict(wl=wl_c, crx=crx_c, cs=cs_c, r1=r1_c, s1=s1_c, r2=r2_c),
    }

    def buf(name, b):
        kind, i = b
        ref = rs_bufs[kind][name]
        return ref if kind == "a" else ref.at[i]

    def number(b):
        kind, i = b
        return {"a": 0, "y": 1, "dp": 3}[kind] + (0 if kind == "a" else i)

    def put_terms(dst, rows, cols, first, second):
        n, w = first.shape[0] // 16, first.shape[1]
        both = jnp.concatenate([first.reshape(n, 2, 8, w), second.reshape(n, 2, 8, w)], axis=2)
        dst[pl.ds(n * rows, n), :, :, cols] = both.astype(BF16)

    def rs_core(b):
        return rcopy(
            buf("wl", b).at[:, 1 - core], buf("crx", b),
            rs_s.at[number(b), 0], rs_r.at[number(b), 0],
            (dp, tm + 1 - 2 * core),
        )

    def part_of(ref, dims, axis, p):
        at = dims.index(axis)
        return ref.at[tuple(slice(None) for _ in range(at)) + (p,)]

    def rs_copies(b, stage):
        src, dst = (("cs", "r1"), ("s1", "r2"), ("s2", "r3"))[stage]
        src, dst = buf(src, b), buf(dst, b)
        kind, n = b[0], number(b)
        axis = {"a": ORDER, "y": ("y", "dp"), "dp": ("dp", "y")}[kind][stage]
        if kind == "a":
            dims = tuple(a for a in ("z", "x", "y") if a not in ORDER[:stage])
        else:
            dims = ("y",) if (kind, stage) == ("dp", 1) else ("z", "x", "y")
        first_sem = {"a": 3, "y": 3, "dp": 15}[kind] * stage
        copies = []
        if axis == "dp":
            for d in range(1, NDP):
                p = (dp + d) % NDP
                copies.append(
                    rcopy(
                        src.at[p // 4, p % 4], dst.at[d - 1],
                        rs_s.at[n, first_sem + d], rs_r.at[n, first_sem + d], (p, tm),
                    )
                )
            return copies, src.at[z, x], dst
        for d in range(1, 4):
            p = (pos[axis] + d) % 4
            copies.append(
                rcopy(
                    part_of(src, dims, axis, p), dst.at[d - 1],
                    rs_s.at[n, first_sem + d], rs_r.at[n, first_sem + d], at_axis(axis, p),
                )
            )
        return copies, part_of(src, dims, axis, pos[axis]), dst

    def stages(b):
        return 3 if b == A else 2

    def rs_one(b):
        rs_core(b).wait_recv()

        @pl.loop(0, 4)
        def _(i):
            rows = pl.ds(i * 16, 16)
            both = buf("wl", b)[rows, core].astype(F32) + buf("crx", b)[rows].astype(F32)
            buf("cs", b)[i] = both.astype(BF16).reshape(4, 4, 16, both.shape[-1])

        for c in rs_copies(b, 0)[0]:
            c.start()

    def rs_next(b, stage):
        copies, own, got = rs_copies(b, stage)
        for c in copies:
            c.wait_recv()
        acc = own[...].astype(F32)
        for d in range(len(copies)):
            acc = acc + got[d].astype(F32)
        if stage < stages(b) - 1:
            buf(("s1", "s2")[stage], b)[...] = acc.astype(BF16)
            for c in rs_copies(b, stage + 1)[0]:
                c.start()
        else:
            acc = acc * SCALE
            if b == A:
                gwo_ref[:, 0:512] = acc[0:8]
                gwo_ref[:, 512:1024] = acc[8:16]
            else:
                c0 = pl.multiple_of(512 * b[1] + (0 if b[0] == "y" else 256), 256)
                gwi_ref[:, pl.ds(c0, 256)] = acc[0:8]
                gwi_ref[:, pl.ds(CH + c0, 256)] = acc[8:16]

    @pl.loop(0, 4)
    def _(n):
        half, i = n // 2, n % 2
        c0 = pl.multiple_of(256 * half, 256)
        rows = jnp.concatenate([sw_v[4 * i + e] for e in range(4)], axis=1)
        put_terms(
            wl_a, i, pl.ds(c0, 256),
            dot_tn(rows, cot[:, pl.ds(c0, 256)]), dot_tn(rows, cot[:, pl.ds(512 + c0, 256)]),
        )

    rs_core(A).start()
    tap_sums(gk1, dsh_v, 2, ar_b[1])
    live_sums()
    rs_one(A)

    grads = ar_b[2]()
    gg_ref[...] = grads[0] * SCALE
    gb_ref[...] = grads[1] * SCALE
    vec[4] = gain_ref[...] * vec[1]
    vec[5] = grads[1] * (1.0 / COUNT)
    vec[6] = grads[0] * (1.0 / COUNT)

    def dconv_rows(parts):
        @pl.loop(0, CB)
        def _(cb):
            factor = vec[4, pl.ds(cb, 1), :]
            shift = vec[5, pl.ds(cb, 1), :]
            tilt = vec[6, pl.ds(cb, 1), :]
            for row0, n in parts:
                rows = pl.ds(row0, n)
                inner = dsh_v[cb, rows, :] - shift - conv_v[cb, rows, :] * tilt
                dcv = jnp.where(live_of(row0, n, 128), factor * inner, 0.0)
                dcv_p[cb, pl.ds(PAD + row0, n), :] = dcv.astype(BF16).astype(F32)

    dconv_rows(((0, PAD), (ROWS - PAD, PAD)))
    halo_d[0]()

    mean, inv_std = vec[0], vec[1]

    def tap_row(k):
        if k == TAPS:
            return jnp.zeros((8, 128), F32)
        tilted = inv_std * (gk3[k + 1] - mean * gk2[k + 1])
        return vec[4] * (gk1[k + 1] - vec[5] * gk2[k + 1] - vec[6] * tilted)

    for k in range(0, 32, 2):
        gkl[k // 2] = jnp.concatenate([tap_row(k), tap_row(k + 1)], axis=0).astype(BF16)

    kt1 = spread("tm", NTM, lambda p: gkl.at[pl.ds(2 * p, 2)], kr1, k1_s, k1_r)
    kt2 = spread("dp", NDP, lambda p: ks1, kr2, k2_s, k2_r)
    kt3 = spread("tm", NTM, lambda p: ks2, kfull, k3_s, k3_r)
    def back_rows(cb, row0, grp):
        acc = taps_pass(dcv_p, cb, row0, lambda o: 32 - o, grp)
        for g in range(0, grp, 2):
            dl, dg = [], []
            for e in (g, g + 1):
                rows = pl.ds(row0 + 8 * e, 8)
                dglu = jnp.where(live_of(row0 + 8 * e, 8, 128), acc[e], 0.0)
                sig = sig_v[cb, rows, :]
                half = dglu * sig
                dl.append(half)
                dg.append(half * lin_v[cb, rows, :] * (1.0 - sig))
            rows = pl.ds(row0 + 8 * g, 16)
            dpre_v[cb, rows, :] = jnp.concatenate(dl, axis=0).astype(BF16)
            dpre_v[CB + cb, rows, :] = jnp.concatenate(dg, axis=0).astype(BF16)

    def pair_terms(j, b):
        first = jnp.concatenate([dpre_v[2 * j], dpre_v[2 * j + 1]], axis=1)
        second = jnp.concatenate([dpre_v[CB + 2 * j], dpre_v[CB + 2 * j + 1]], axis=1)

        @pl.loop(0, 2)
        def _(i):
            rows = feats[:, pl.ds(pl.multiple_of(512 * i, 512), 512)]
            put_terms(buf("wl", b), i, slice(None), dot_tn(rows, first), dot_tn(rows, second))

        rs_core(b).start()

    def kt_sum(n):
        if n == 0:
            kr1[tm] = gkl[pl.ds(2 * tm, 2)]
            kt1[0]()
        elif n == 1:
            kt1[1]()
            v = total(kr1, NTM).astype(BF16)
            ks1[...] = v
            kr2[dp] = v
            kt2[0]()
        elif n == 2:
            kt2[1]()
            v = total(kr2, NDP)
            ks2[...] = v
            kfull[tm] = v
            kt3[0]()
        else:
            kt3[1]()
            for cb in range(CB):
                for k in range(TAPS):
                    at = 8 * (k % 2) + cb
                    row = kfull[k // 4, k % 4 // 2, at : at + 1, :]
                    gk_ref[k : k + 1, 128 * cb : 128 * cb + 128] = row * SCALE

    def frame_cols(j):
        c0 = pl.multiple_of(256 * j, 256)
        rows = jnp.concatenate([dpre_v[c] for c in range(2 * CB)], axis=1)
        out_v[1, :, pl.ds(c0, 256)] = dot_nt(rows, w_in[pl.ds(c0, 256), :]).astype(BF16)

    def out_cols(j):
        c0 = pl.multiple_of(256 * j, 256)
        rows = jnp.concatenate([sw_v[cb] for cb in range(CB)], axis=1)
        out_v[0, :, pl.ds(c0, 256)] = dot_nn(rows, w_out[:, pl.ds(c0, 256)]).astype(BF16)

    kt_sum(0)
    dconv_rows(((PAD, 384), (PAD + 384, 352)))

    def back_pair(j, at_row):
        @pl.loop(0, 6)
        def _(i):
            at_row(i)
            row0 = pl.multiple_of((i + 1) % 6 * 128, 128)

            @pl.loop(0, 2)
            def _(h):
                back_rows(2 * j + h, row0, 16)

    @pl.loop(0, 2)
    def _(n):
        def even(i):
            pl.when((n == 0) & (i == 4))(halo_d[1])
            pl.when((n == 1) & (i == 5))(lambda: rs_one(("dp", 0)))

        def odd(i):
            pl.when(i == 5)(lambda: rs_one(("y", n)))

        back_pair(2 * n, even)
        pair_terms(2 * n, ("y", n))
        pl.when(n == 0)(lambda: kt_sum(1))
        back_pair(2 * n + 1, odd)
        pair_terms(2 * n + 1, ("dp", n))
        pl.when(n == 0)(lambda: kt_sum(2))
        pl.when(n == 1)(lambda: rs_next(A, 0))

    @pl.loop(0, 8)
    def _(n):
        pl.when(n < 4)(lambda: frame_cols(n))
        pl.when(n >= 4)(lambda: out_cols(n - 4))
        pl.when(n == 0)(lambda: rs_one(("dp", 1)))
        pl.when(n == 4)(lambda: rs_next(A, 1))
        pl.when((n == 3) | (n == 7))(lambda: rs_next(("y", n // 4), 0))
        pl.when(n == 5)(lambda: rs_next(("dp", 0), 0))

    gf_copy = pltpu.make_async_copy(out_v.at[1], gf_h, out_sem.at[1])
    gf_copy.start()
    out_copy = pltpu.make_async_copy(out_v.at[0], out_h, out_sem.at[0])
    out_copy.start()
    rs_next(("dp", 1), 0)
    kt_sum(3)
    rs_next(A, 2)

    @pl.loop(0, 2)
    def _(n):
        rs_next(("y", n), 1)
        rs_next(("dp", n), 1)

    for t in (halo_g, halo_d, kt1, kt2, kt3):
        t[2]()
    ar_a[3]()
    ar_b[3]()
    def block_sent(b):
        rs_core(b).wait_send()
        for stage in range(stages(b)):
            for c in rs_copies(b, stage)[0]:
                c.wait_send()

    block_sent(A)

    @pl.loop(0, 2)
    def _(n):
        block_sent(("y", n))
        block_sent(("dp", n))

    out_copy.wait()
    gf_copy.wait()


SCALE = 1.0 / math.sqrt(16 * 6144)


def rs_scratch(kind):
    shapes = [(64, 2), (64,), (4, 4, 4)]
    shapes += {
        "a": [(3, 4, 4), (4, 4), (3, 4), (4,), (3,)],
        "y": [(3, 4, 4), (4, 4), (15,)],
        "dp": [(15, 4), (4,), (3,)],
    }[kind]
    lead, width = ((), 512) if kind == "a" else ((2,), 256)
    return [pltpu.VMEM((*lead, *s, 16, width), BF16) for s in shapes]


PIECES = ((0, 4), (1, 4), (2, 1), (3, 1), (4, 1), (5, 1), (6, 1))


def hand_over(*refs):
    srcs, dsts, held, sems = refs[0:7], refs[7:14], refs[14:21], refs[21]
    steps = []
    for i, parts in PIECES:
        rows = srcs[i].shape[0] // parts
        for p in range(parts):
            at = (pl.ds(p * rows, rows),)
            n = len(steps)
            steps.append((
                pltpu.make_async_copy(srcs[i].at[at], held[i].at[at], sems.at[n, 0]),
                pltpu.make_async_copy(held[i].at[at], dsts[i].at[at], sems.at[n, 1]),
            ))
    for come, _ in steps:
        come.start()
    for come, go in steps:
        come.wait()
        go.start()
    for _, go in steps:
        go.wait()


def local(frames, lengths, w_in, w_dw, bn_gain, bn_bias, w_out, cotangent):
    hbm = pl.BlockSpec(memory_space=pl.ANY)
    vmem = pl.BlockSpec(memory_space=pltpu.VMEM)
    smem = pl.BlockSpec(memory_space=pltpu.SMEM)
    dma = pltpu.SemaphoreType.DMA
    outs = pl.pallas_call(
        kernel,
        out_shape=(
            jax.ShapeDtypeStruct((ROWS, CH), BF16),
            jax.ShapeDtypeStruct((ROWS, CH), BF16),
            jax.ShapeDtypeStruct((8, 2 * CH), F32),
            jax.ShapeDtypeStruct((8, CH), F32),
            jax.ShapeDtypeStruct((TAPS, CH), F32),
            jax.ShapeDtypeStruct((8, 128), F32),
            jax.ShapeDtypeStruct((8, 128), F32),
        ),
        in_specs=[smem, hbm, hbm, vmem, vmem, vmem, hbm, hbm],
        out_specs=(hbm, hbm, vmem, vmem, vmem, vmem, vmem),
        scratch_shapes=[
            pltpu.VMEM((ROWS, CH), BF16),
            pltpu.VMEM((CH, 2 * CH), BF16),
            pltpu.VMEM((CH, CH), BF16),
            pltpu.VMEM((ROWS, CH), BF16),
            pltpu.VMEM((CB, 2, 8, 128), F32),
            pltpu.VMEM((CB, ROWS, 128), F32),
            pltpu.VMEM((CB, ROWS, 128), F32),
            pltpu.VMEM((CB, PROWS, 128), F32),
            pltpu.VMEM((CB, PROWS, 128), F32),
            pltpu.VMEM((CB, ROWS, 128), F32),
            pltpu.VMEM((CB, ROWS, 128), F32),
            pltpu.VMEM((CB, ROWS, 128), BF16),
            pltpu.VMEM((2 * CB, ROWS, 128), BF16),
            pltpu.VMEM((2, ROWS, CH), BF16),
            pltpu.VMEM((CB, 32, 8, 128), F32),
            pltpu.VMEM((8, 8, 128), F32),
            pltpu.VMEM((2, 8, 128), F32),
            pltpu.VMEM((2, 2, 8, 128), F32),
            pltpu.VMEM((2, 2, 8, 128), F32),
            pltpu.VMEM((2, NTM, 2, 8, 128), F32),
            pltpu.VMEM((2, NDP, 2, 8, 128), F32),
            pltpu.VMEM((16, 16, 128), BF16),
            pltpu.VMEM((32, 8, 128), F32),
            pltpu.VMEM((32, 8, 128), F32),
            pltpu.VMEM((32, 8, 128), F32),
            pltpu.VMEM((NTM, 2, 16, 128), BF16),
            pltpu.VMEM((2, 16, 128), BF16),
            pltpu.VMEM((NDP, 2, 16, 128), BF16),
            pltpu.VMEM((2, 16, 128), F32),
            pltpu.VMEM((NTM, 2, 16, 128), F32),
            *rs_scratch("a"),
            *rs_scratch("y"),
            *rs_scratch("dp"),
            dma((3,)),
            dma((4, 2)),
            dma((2,)),
            dma((4,)),
            dma((4,)),
            dma((2, NTM)),
            dma((2, NTM)),
            dma((2, NDP)),
            dma((2, NDP)),
            dma((NTM,)),
            dma((NTM,)),
            dma((NDP,)),
            dma((NDP,)),
            dma((NTM,)),
            dma((NTM,)),
            dma((NB, 19)),
            dma((NB, 19)),
        ],
        compiler_params=pltpu.CompilerParams(
            collective_id=0, has_side_effects=True, vmem_limit_bytes=62 << 20
        ),
        name="conformer_conv",
    )(
        lengths, frames[0], w_in, w_dw, bn_gain.reshape(8, 128), bn_bias.reshape(8, 128),
        w_out, cotangent[0],
    )
    out, gf, gwi, gwo, gk, gg, gb = pl.pallas_call(
        hand_over,
        out_shape=tuple(jax.ShapeDtypeStruct(o.shape, o.dtype) for o in outs),
        in_specs=[hbm] * 7,
        out_specs=(hbm,) * 7,
        scratch_shapes=[pltpu.VMEM(o.shape, o.dtype) for o in outs] + [dma((13, 2))],
        name="hand_over",
    )(*outs)
    return (out[None], gf[None], gwi, gwo, gk, gg.reshape(CH), gb.reshape(CH))


def solution(mesh):
    placed = (P("dp", "tm", None), P("dp"), P(), P(), P(), P(), P(), P("dp", "tm", None))
    return jax.shard_map(
        local,
        mesh=mesh,
        in_specs=placed,
        out_specs=(
            P("dp", "tm", None),
            P("dp", "tm", None),
            P(("dp", "tm"), None),
            P(("dp", "tm"), None),
            P(),
            P(),
            P(),
        ),
        check_vma=False,
    )
```

```python
import math

import jax
import jax.numpy as jnp
from jax import lax
from jax.experimental import pallas as pl
from jax.experimental.pallas import tpu as pltpu
from jax.sharding import PartitionSpec as P

MESH_ID = pl.DeviceIdType.MESH
F32 = jnp.float32
BF16 = jnp.bfloat16

ROWS = 768
CH = 1024
CB = 8
PAD = 16
PROWS = ROWS + 2 * PAD
TAPS = 31
COUNT = 58982.0
NDP, NTM = 16, 8
GRP = 12
GROUPS = ROWS // (8 * GRP)
NB = 5
ORDER = ("z", "x", "y")


def sigmoid(x):
    return 0.5 * jnp.tanh(0.5 * x) + 0.5


def dot_nn(a, b):
    return lax.dot_general(a, b, (((1,), (0,)), ((), ())), preferred_element_type=F32)


def dot_tn(a, b):
    return lax.dot_general(a, b, (((0,), (0,)), ((), ())), preferred_element_type=F32)


def dot_nt(a, b):
    return lax.dot_general(a, b, (((1,), (1,)), ((), ())), preferred_element_type=F32)


def kernel(
    len_ref, frames_h, w_in_h, w_dw, gain_ref, bias_ref, w_out_h, cot_h,
    out_h, gf_h, gwi_ref, gwo_ref, gk_ref, gg_ref, gb_ref,
    feats, w_in, w_out, cot, stat_v, lin_v, sig_v, glu_p, dcv_p, conv_v, dsh_v,
    sw_v, dpre_v, out_v, wb, vec,
    red, red_in, red_mid, red_rx1, red_rx2,
    gkl, gk1, gk2, gk3, kr1, ks1, kr2, ks2, kfull,
    wl_a, crx_a, cs_a, r1_a, s1_a, r2_a, s2_a, r3_a,
    wl_b, crx_b, cs_b, r1_b, s1_b, r2_b,
    wl_c, crx_c, cs_c, r1_c, s1_c, r2_c,
    in_sem, w_sem, out_sem, halo_s, halo_r, ar1_s, ar1_r, ar2_s, ar2_r,
    k1_s, k1_r, k2_s, k2_r, k3_s, k3_r, rs_s, rs_r,
):
    dp = lax.axis_index("dp")
    tm = lax.axis_index("tm")
    z, x = dp // 4, dp % 4
    y, core = tm // 2, tm % 2
    pos = {"z": z, "x": x, "y": y}

    def at_axis(axis, p):
        if axis == "z":
            return (p * 4 + x, tm)
        if axis == "x":
            return (z * 4 + p, tm)
        return (dp, p * 2 + core)

    def rcopy(src, dst, ss, rs, dev):
        return pltpu.make_async_remote_copy(
            src_ref=src, dst_ref=dst, send_sem=ss, recv_sem=rs,
            device_id=dev, device_id_type=MESH_ID,
        )

    def w_in_load(j, half):
        cols = pl.ds(half * CH + j * 256, 256)
        return pltpu.make_async_copy(w_in_h.at[:, cols], w_in.at[:, cols], w_sem.at[j, half])

    loads = [
        pltpu.make_async_copy(frames_h, feats, in_sem.at[0]),
        pltpu.make_async_copy(cot_h, cot, in_sem.at[1]),
        pltpu.make_async_copy(w_out_h, w_out, in_sem.at[2]),
    ]
    loads[0].start()
    for j in range(4):
        for half in range(2):
            w_in_load(j, half).start()
    loads[1].start()
    loads[2].start()
    barrier = pltpu.get_barrier_semaphore()
    for d in range(1, NTM):
        pl.semaphore_signal(barrier, inc=1, device_id=(dp, (tm + d) % NTM), device_id_type=MESH_ID)
    for d in range(1, NDP):
        pl.semaphore_signal(barrier, inc=1, device_id=((dp + d) % NDP, tm), device_id_type=MESH_ID)

    limit = len_ref[0] - tm * ROWS

    def live_of(row0, rows, cols):
        t = lax.broadcasted_iota(jnp.int32, (rows, cols), 0) + row0
        return t < limit

    @pl.loop(0, TAPS)
    def _(k):
        row = w_dw[pl.ds(k, 1), :]
        for cb in range(CB):
            wb[cb, k + 1] = jnp.broadcast_to(row[:, cb * 128 : cb * 128 + 128], (8, 128))

    for ref in (glu_p, dcv_p):
        @pl.when(tm == 0)
        def _():
            ref[:, 0:PAD, :] = jnp.zeros((CB, PAD, 128), F32)

        @pl.when(tm == NTM - 1)
        def _():
            ref[:, PAD + ROWS : PROWS, :] = jnp.zeros((CB, PAD, 128), F32)

    loads[0].wait()

    @pl.loop(0, 4)
    def _(j):
        c0 = pl.multiple_of(j * 256, 256)
        w_in_load(j, 0).wait()
        w_in_load(j, 1).wait()
        rows = feats[...]
        lin = dot_nn(rows, w_in[:, pl.ds(c0, 256)])
        sig = sigmoid(dot_nn(rows, w_in[:, pl.ds(CH + c0, 256)]))
        glu = jnp.where(live_of(0, ROWS, 256), lin * sig, 0.0).astype(BF16).astype(F32)
        for h in range(2):
            cols = slice(h * 128, h * 128 + 128)
            lin_v[2 * j + h] = lin[:, cols]
            sig_v[2 * j + h] = sig[:, cols]
            glu_p[2 * j + h, pl.ds(PAD, ROWS), :] = glu[:, cols]

    def halo(ref, n):
        to_left = rcopy(
            ref.at[:, pl.ds(PAD, PAD), :], ref.at[:, pl.ds(PAD + ROWS, PAD), :],
            halo_s.at[n], halo_r.at[n], (dp, (tm + NTM - 1) % NTM),
        )
        to_right = rcopy(
            ref.at[:, pl.ds(ROWS, PAD), :], ref.at[:, pl.ds(0, PAD), :],
            halo_s.at[n + 1], halo_r.at[n + 1], (dp, (tm + 1) % NTM),
        )

        def start():
            pl.when(tm > 0)(to_left.start)
            pl.when(tm < NTM - 1)(to_right.start)

        def recv():
            pl.when(tm < NTM - 1)(to_left.wait_recv)
            pl.when(tm > 0)(to_right.wait_recv)

        def sent():
            pl.when(tm > 0)(to_left.wait_send)
            pl.when(tm < NTM - 1)(to_right.wait_send)

        return start, recv, sent

    halo_g, halo_d = halo(glu_p, 0), halo(dcv_p, 2)
    def taps_pass(src, cb, row0, tap_of, grp):
        acc = [None] * grp
        for r in range(8):
            xs = [src[cb, pl.ds(row0 + (8 * n + r), 8), :] for n in range(grp + 3)]
            for q in range(4):
                o = 8 * q + r
                if o == 0:
                    continue
                w = wb[cb, tap_of(o)]
                for g in range(grp):
                    term = w * xs[g + q]
                    acc[g] = term if acc[g] is None else acc[g] + term
        return acc

    def conv_rows(cb, row0, grp, carry):
        s, sq = carry
        acc = taps_pass(glu_p, cb, row0, lambda o: o, grp)
        for g in range(grp):
            kept = jnp.where(live_of(row0 + 8 * g, 8, 128), acc[g], 0.0)
            conv_v[cb, pl.ds(row0 + 8 * g, 8), :] = kept
            s = s + kept
            sq = sq + kept * kept
        return s, sq

    EDGE, INNER = 8, 16

    def conv_inner(cb):
        def step(i, carry):
            return conv_rows(cb, pl.multiple_of(64 + i * 128, 64), INNER, carry)

        zero = jnp.zeros((8, 128), F32)
        s, sq = lax.fori_loop(0, (ROWS - 128) // 128, step, (zero, zero))
        stat_v[cb, 0] = s
        stat_v[cb, 1] = sq

    def meet():
        pl.semaphore_wait(barrier, NTM + NDP - 2)
        halo_g[0]()

    @pl.loop(0, CB)
    def _(cb):
        pl.when(cb == 2)(meet)
        conv_inner(cb)

    halo_g[1]()

    @pl.loop(0, CB)
    def _(cb):
        def step(i, carry):
            return conv_rows(cb, pl.multiple_of(i * (ROWS - 64), 64), EDGE, carry)

        s, sq = lax.fori_loop(0, 2, step, (stat_v[cb, 0], stat_v[cb, 1]))
        red[0, pl.ds(cb, 1), :] = jnp.sum(s, axis=0, keepdims=True)
        red[1, pl.ds(cb, 1), :] = jnp.sum(sq, axis=0, keepdims=True)

    def spread(axis, count, src_of, dst, ss, rs):
        me = tm if axis == "tm" else dp

        def copy(d, slot):
            peer = (me + d) % count
            dev = (dp, peer) if axis == "tm" else (peer, tm)
            return rcopy(src_of(peer), dst.at[slot], ss.at[d], rs.at[slot], dev)

        def start():
            for d in range(1, count):
                copy(d, me).start()

        def recv():
            for d in range(1, count):
                copy(d, (me + d) % count).wait_recv()

        def sent():
            for d in range(1, count):
                copy(d, me).wait_send()

        return start, recv, sent

    def total(ref, count):
        acc = ref[0].astype(F32)
        for i in range(1, count):
            acc = acc + ref[i].astype(F32)
        return acc

    def all_sum(n):
        one = spread("tm", NTM, lambda p: red_in.at[n], red_rx1.at[n], ar1_s.at[n], ar1_r.at[n])
        two = spread("dp", NDP, lambda p: red_mid.at[n], red_rx2.at[n], ar2_s.at[n], ar2_r.at[n])

        def begin():
            v = red[...]
            red_in[n] = v
            red_rx1[n, tm] = v
            one[0]()

        def middle():
            one[1]()
            v = total(red_rx1.at[n], NTM)
            red_mid[n] = v
            red_rx2[n, dp] = v
            two[0]()

        def end():
            two[1]()
            return total(red_rx2.at[n], NDP)

        def sent():
            one[2]()
            two[2]()

        return begin, middle, end, sent

    ar_a, ar_b = all_sum(0), all_sum(1)
    ar_a[0]()

    loads[1].wait()
    loads[2].wait()

    @pl.loop(0, 4)
    def _(j):
        c0 = pl.multiple_of(j * 256, 256)
        ds = dot_nt(cot[...], w_out[pl.ds(c0, 256), :])
        for h in range(2):
            dsh_v[2 * j + h] = ds[:, h * 128 : h * 128 + 128]

    def tap_sums(dst, grad, *between):
        grp = 16

        @pl.loop(0, CB)
        def _(cb):
            for blocks, call in between:
                pl.when(cb == blocks)(call)

            def step(i, accs):
                row0 = pl.multiple_of(i * (8 * grp), 8 * grp)
                accs = list(accs)
                ds = [grad[cb, pl.ds(row0 + 8 * g, 8), :] for g in range(grp)]
                for r in range(8):
                    xs = [glu_p[cb, pl.ds(row0 + (8 * n + r), 8), :] for n in range(grp + 3)]
                    for q in range(4):
                        o = 8 * q + r
                        if o == 0:
                            continue
                        for g in range(grp):
                            accs[o - 1] = accs[o - 1] + xs[g + q] * ds[g]
                return tuple(accs)

            zero = jnp.zeros((8, 128), F32)
            accs = lax.fori_loop(0, ROWS // (8 * grp), step, (zero,) * TAPS)
            for k in range(TAPS):
                dst[k + 1, pl.ds(cb, 1), :] = jnp.sum(accs[k], axis=0, keepdims=True)

    def window(rows_of):
        count = jnp.clip(limit, 0, ROWS)
        row, tap = rows_of
        return ((row >= tap) & (row < count + tap)).astype(F32).astype(BF16)

    def live_sums():
        def grid(n):
            return [lax.broadcasted_iota(jnp.int32, (32, n), d) for d in (1, 0)]

        row, tap = grid(ROWS)
        inner = window((row + PAD, tap))
        row, tap = grid(2 * PAD)
        outer = window((jnp.where(row < PAD, row, row + ROWS), tap))
        for cb in range(CB):
            ends = jnp.concatenate(
                [glu_p[cb, 0:PAD, :], glu_p[cb, PAD + ROWS : PROWS, :]], axis=0
            )
            gk2[:, cb, :] = dot_nn(inner, glu_p[cb, PAD : PAD + ROWS, :].astype(BF16)) + dot_nn(
                outer, ends.astype(BF16)
            )

    tap_sums(gk3, conv_v, (1, ar_a[1]))
    sums = ar_a[2]()
    mean = sums[0] * (1.0 / COUNT)
    variance = sums[1] * (1.0 / COUNT) - mean * mean
    inv_std = lax.rsqrt(variance + 1e-05)
    vec[0] = mean
    vec[1] = inv_std
    vec[2] = gain_ref[...]
    vec[3] = bias_ref[...]

    @pl.loop(0, CB)
    def _(cb):
        mean_r = vec[0, pl.ds(cb, 1), :]
        inv_r = vec[1, pl.ds(cb, 1), :]
        gain_r = vec[2, pl.ds(cb, 1), :]
        bias_r = vec[3, pl.ds(cb, 1), :]

        def step(i, carry):
            sg, sb = carry
            n = 256
            row0 = pl.multiple_of(i * n, n)
            live = live_of(row0, n, 128)
            normed = (conv_v[cb, pl.ds(row0, n), :] - mean_r) * inv_r
            shifted = gain_r * normed + bias_r
            act = sigmoid(shifted)
            sw_v[cb, pl.ds(row0, n), :] = jnp.where(live, shifted * act, 0.0).astype(BF16)
            slope = act * (1.0 + shifted * (1.0 - act))
            dsh = jnp.where(live, dsh_v[cb, pl.ds(row0, n), :] * slope, 0.0)
            dsh_v[cb, pl.ds(row0, n), :] = dsh
            conv_v[cb, pl.ds(row0, n), :] = normed
            prod = dsh * normed
            for g in range(n // 8):
                sg = sg + prod[8 * g : 8 * g + 8]
                sb = sb + dsh[8 * g : 8 * g + 8]
            return sg, sb

        zero = jnp.zeros((8, 128), F32)
        sg, sb = lax.fori_loop(0, ROWS // 256, step, (zero, zero))
        red[0, pl.ds(cb, 1), :] = jnp.sum(sg, axis=0, keepdims=True)
        red[1, pl.ds(cb, 1), :] = jnp.sum(sb, axis=0, keepdims=True)

    ar_b[0]()

    A = ("a", None)
    rs_bufs = {
        "a": dict(wl=wl_a, crx=crx_a, cs=cs_a, r1=r1_a, s1=s1_a, r2=r2_a, s2=s2_a, r3=r3_a),
        "y": dict(wl=wl_b, crx=crx_b, cs=cs_b, r1=r1_b, s1=s1_b, r2=r2_b),
        "dp": dict(wl=wl_c, crx=crx_c, cs=cs_c, r1=r1_c, s1=s1_c, r2=r2_c),
    }

    def buf(name, b):
        kind, i = b
        ref = rs_bufs[kind][name]
        return ref if kind == "a" else ref.at[i]

    def number(b):
        kind, i = b
        return {"a": 0, "y": 1, "dp": 3}[kind] + (0 if kind == "a" else i)

    def put_terms(dst, rows, cols, first, second):
        n, w = first.shape[0] // 16, first.shape[1]
        both = jnp.concatenate([first.reshape(n, 2, 8, w), second.reshape(n, 2, 8, w)], axis=2)
        dst[pl.ds(n * rows, n), :, :, cols] = both.astype(BF16)

    def rs_core(b):
        return rcopy(
            buf("wl", b).at[:, 1 - core], buf("crx", b),
            rs_s.at[number(b), 0], rs_r.at[number(b), 0],
            (dp, tm + 1 - 2 * core),
        )

    def part_of(ref, dims, axis, p):
        at = dims.index(axis)
        return ref.at[tuple(slice(None) for _ in range(at)) + (p,)]

    def rs_copies(b, stage):
        src, dst = (("cs", "r1"), ("s1", "r2"), ("s2", "r3"))[stage]
        src, dst = buf(src, b), buf(dst, b)
        kind, n = b[0], number(b)
        axis = {"a": ORDER, "y": ("y", "dp"), "dp": ("dp", "y")}[kind][stage]
        if kind == "a":
            dims = tuple(a for a in ("z", "x", "y") if a not in ORDER[:stage])
        else:
            dims = ("y",) if (kind, stage) == ("dp", 1) else ("z", "x", "y")
        first_sem = {"a": 3, "y": 3, "dp": 15}[kind] * stage
        copies = []
        if axis == "dp":
            for d in range(1, NDP):
                p = (dp + d) % NDP
                copies.append(
                    rcopy(
                        src.at[p // 4, p % 4], dst.at[d - 1],
                        rs_s.at[n, first_sem + d], rs_r.at[n, first_sem + d], (p, tm),
                    )
                )
            return copies, src.at[z, x], dst
        for d in range(1, 4):
            p = (pos[axis] + d) % 4
            copies.append(
                rcopy(
                    part_of(src, dims, axis, p), dst.at[d - 1],
                    rs_s.at[n, first_sem + d], rs_r.at[n, first_sem + d], at_axis(axis, p),
                )
            )
        return copies, part_of(src, dims, axis, pos[axis]), dst

    def stages(b):
        return 3 if b == A else 2

    def rs_one(b):
        rs_core(b).wait_recv()

        @pl.loop(0, 4)
        def _(i):
            rows = pl.ds(i * 16, 16)
            both = buf("wl", b)[rows, core].astype(F32) + buf("crx", b)[rows].astype(F32)
            buf("cs", b)[i] = both.astype(BF16).reshape(4, 4, 16, both.shape[-1])

        for c in rs_copies(b, 0)[0]:
            c.start()

    def rs_next(b, stage):
        copies, own, got = rs_copies(b, stage)
        for c in copies:
            c.wait_recv()
        acc = own[...].astype(F32)
        for d in range(len(copies)):
            acc = acc + got[d].astype(F32)
        if stage < stages(b) - 1:
            buf(("s1", "s2")[stage], b)[...] = acc.astype(BF16)
            for c in rs_copies(b, stage + 1)[0]:
                c.start()
        else:
            acc = acc * SCALE
            if b == A:
                gwo_ref[:, 0:512] = acc[0:8]
                gwo_ref[:, 512:1024] = acc[8:16]
            else:
                c0 = pl.multiple_of(512 * b[1] + (0 if b[0] == "y" else 256), 256)
                gwi_ref[:, pl.ds(c0, 256)] = acc[0:8]
                gwi_ref[:, pl.ds(CH + c0, 256)] = acc[8:16]

    @pl.loop(0, 4)
    def _(n):
        half, i = n // 2, n % 2
        c0 = pl.multiple_of(256 * half, 256)
        rows = jnp.concatenate([sw_v[4 * i + e] for e in range(4)], axis=1)
        put_terms(
            wl_a, i, pl.ds(c0, 256),
            dot_tn(rows, cot[:, pl.ds(c0, 256)]), dot_tn(rows, cot[:, pl.ds(512 + c0, 256)]),
        )

    rs_core(A).start()
    tap_sums(gk1, dsh_v, (2, ar_b[1]), (5, lambda: rs_one(A)))
    live_sums()

    grads = ar_b[2]()
    gg_ref[...] = grads[0] * SCALE
    gb_ref[...] = grads[1] * SCALE
    vec[4] = gain_ref[...] * vec[1]
    vec[5] = grads[1] * (1.0 / COUNT)
    vec[6] = grads[0] * (1.0 / COUNT)

    def dconv_rows(parts):
        @pl.loop(0, CB)
        def _(cb):
            factor = vec[4, pl.ds(cb, 1), :]
            shift = vec[5, pl.ds(cb, 1), :]
            tilt = vec[6, pl.ds(cb, 1), :]
            for row0, n in parts:
                rows = pl.ds(row0, n)
                inner = dsh_v[cb, rows, :] - shift - conv_v[cb, rows, :] * tilt
                dcv = jnp.where(live_of(row0, n, 128), factor * inner, 0.0)
                dcv_p[cb, pl.ds(PAD + row0, n), :] = dcv.astype(BF16).astype(F32)

    dconv_rows(((0, PAD), (ROWS - PAD, PAD)))
    halo_d[0]()

    mean, inv_std = vec[0], vec[1]

    def tap_row(k):
        if k == TAPS:
            return jnp.zeros((8, 128), F32)
        tilted = inv_std * (gk3[k + 1] - mean * gk2[k + 1])
        return vec[4] * (gk1[k + 1] - vec[5] * gk2[k + 1] - vec[6] * tilted)

    for k in range(0, 32, 2):
        gkl[k // 2] = jnp.concatenate([tap_row(k), tap_row(k + 1)], axis=0).astype(BF16)

    kt1 = spread("tm", NTM, lambda p: gkl.at[pl.ds(2 * p, 2)], kr1, k1_s, k1_r)
    kt2 = spread("dp", NDP, lambda p: ks1, kr2, k2_s, k2_r)
    kt3 = spread("tm", NTM, lambda p: ks2, kfull, k3_s, k3_r)
    def back_rows(cb, row0, grp):
        acc = taps_pass(dcv_p, cb, row0, lambda o: 32 - o, grp)
        for g in range(0, grp, 2):
            dl, dg = [], []
            for e in (g, g + 1):
                rows = pl.ds(row0 + 8 * e, 8)
                dglu = jnp.where(live_of(row0 + 8 * e, 8, 128), acc[e], 0.0)
                sig = sig_v[cb, rows, :]
                half = dglu * sig
                dl.append(half)
                dg.append(half * lin_v[cb, rows, :] * (1.0 - sig))
            rows = pl.ds(row0 + 8 * g, 16)
            dpre_v[cb, rows, :] = jnp.concatenate(dl, axis=0).astype(BF16)
            dpre_v[CB + cb, rows, :] = jnp.concatenate(dg, axis=0).astype(BF16)

    def pair_terms(j, b):
        first = jnp.concatenate([dpre_v[2 * j], dpre_v[2 * j + 1]], axis=1)
        second = jnp.concatenate([dpre_v[CB + 2 * j], dpre_v[CB + 2 * j + 1]], axis=1)

        @pl.loop(0, 2)
        def _(i):
            rows = feats[:, pl.ds(pl.multiple_of(512 * i, 512), 512)]
            put_terms(buf("wl", b), i, slice(None), dot_tn(rows, first), dot_tn(rows, second))

        rs_core(b).start()

    def kt_sum(n):
        if n == 0:
            kr1[tm] = gkl[pl.ds(2 * tm, 2)]
            kt1[0]()
        elif n == 1:
            kt1[1]()
            v = total(kr1, NTM).astype(BF16)
            ks1[...] = v
            kr2[dp] = v
            kt2[0]()
        elif n == 2:
            kt2[1]()
            v = total(kr2, NDP)
            ks2[...] = v
            kfull[tm] = v
            kt3[0]()
        else:
            kt3[1]()
            for cb in range(CB):
                for k in range(TAPS):
                    at = 8 * (k % 2) + cb
                    row = kfull[k // 4, k % 4 // 2, at : at + 1, :]
                    gk_ref[k : k + 1, 128 * cb : 128 * cb + 128] = row * SCALE

    def frame_cols(j):
        c0 = pl.multiple_of(256 * j, 256)
        rows = jnp.concatenate([dpre_v[c] for c in range(2 * CB)], axis=1)
        out_v[1, :, pl.ds(c0, 256)] = dot_nt(rows, w_in[pl.ds(c0, 256), :]).astype(BF16)

    def out_cols(j):
        c0 = pl.multiple_of(256 * j, 256)
        rows = jnp.concatenate([sw_v[cb] for cb in range(CB)], axis=1)
        out_v[0, :, pl.ds(c0, 256)] = dot_nn(rows, w_out[:, pl.ds(c0, 256)]).astype(BF16)

    kt_sum(0)
    dconv_rows(((PAD, 384), (PAD + 384, 352)))

    def back_pair(j, at_row):
        @pl.loop(0, 6)
        def _(i):
            at_row(i)
            row0 = pl.multiple_of((i + 1) % 6 * 128, 128)

            @pl.loop(0, 2)
            def _(h):
                back_rows(2 * j + h, row0, 16)

    @pl.loop(0, 2)
    def _(n):
        def even(i):
            pl.when((n == 0) & (i == 4))(halo_d[1])
            pl.when((n == 1) & (i == 5))(lambda: rs_one(("dp", 0)))

        def odd(i):
            pl.when(i == 5)(lambda: rs_one(("y", n)))

        back_pair(2 * n, even)
        pair_terms(2 * n, ("y", n))
        pl.when(n == 0)(lambda: kt_sum(1))
        back_pair(2 * n + 1, odd)
        pair_terms(2 * n + 1, ("dp", n))
        pl.when(n == 0)(lambda: kt_sum(2))
        pl.when(n == 0)(lambda: rs_next(A, 0))
        pl.when(n == 1)(lambda: rs_next(A, 1))

    @pl.loop(0, 8)
    def _(n):
        pl.when(n < 4)(lambda: frame_cols(n))
        pl.when(n >= 4)(lambda: out_cols(n - 4))
        pl.when(n == 0)(lambda: rs_one(("dp", 1)))
        pl.when(n == 4)(lambda: rs_next(A, 2))
        pl.when((n == 3) | (n == 7))(lambda: rs_next(("y", n // 4), 0))
        pl.when(n == 5)(lambda: rs_next(("dp", 0), 0))

    gf_copy = pltpu.make_async_copy(out_v.at[1], gf_h, out_sem.at[1])
    gf_copy.start()
    out_copy = pltpu.make_async_copy(out_v.at[0], out_h, out_sem.at[0])
    out_copy.start()
    rs_next(("dp", 1), 0)
    kt_sum(3)

    @pl.loop(0, 2)
    def _(n):
        rs_next(("y", n), 1)
        rs_next(("dp", n), 1)

    for t in (halo_g, halo_d, kt1, kt2, kt3):
        t[2]()
    ar_a[3]()
    ar_b[3]()
    def block_sent(b):
        rs_core(b).wait_send()
        for stage in range(stages(b)):
            for c in rs_copies(b, stage)[0]:
                c.wait_send()

    block_sent(A)

    @pl.loop(0, 2)
    def _(n):
        block_sent(("y", n))
        block_sent(("dp", n))

    out_copy.wait()
    gf_copy.wait()


SCALE = 1.0 / math.sqrt(16 * 6144)


def rs_scratch(kind):
    shapes = [(64, 2), (64,), (4, 4, 4)]
    shapes += {
        "a": [(3, 4, 4), (4, 4), (3, 4), (4,), (3,)],
        "y": [(3, 4, 4), (4, 4), (15,)],
        "dp": [(15, 4), (4,), (3,)],
    }[kind]
    lead, width = ((), 512) if kind == "a" else ((2,), 256)
    return [pltpu.VMEM((*lead, *s, 16, width), BF16) for s in shapes]


PIECES = ((0, 4), (1, 4), (2, 1), (3, 1), (4, 1), (5, 1), (6, 1))


def hand_over(*refs):
    srcs, dsts, held, sems = refs[0:7], refs[7:14], refs[14:21], refs[21]
    steps = []
    for i, parts in PIECES:
        rows = srcs[i].shape[0] // parts
        for p in range(parts):
            at = (pl.ds(p * rows, rows),)
            n = len(steps)
            steps.append((
                pltpu.make_async_copy(srcs[i].at[at], held[i].at[at], sems.at[n, 0]),
                pltpu.make_async_copy(held[i].at[at], dsts[i].at[at], sems.at[n, 1]),
            ))
    for come, _ in steps:
        come.start()
    for come, go in steps:
        come.wait()
        go.start()
    for _, go in steps:
        go.wait()


def local(frames, lengths, w_in, w_dw, bn_gain, bn_bias, w_out, cotangent):
    hbm = pl.BlockSpec(memory_space=pl.ANY)
    vmem = pl.BlockSpec(memory_space=pltpu.VMEM)
    smem = pl.BlockSpec(memory_space=pltpu.SMEM)
    dma = pltpu.SemaphoreType.DMA
    outs = pl.pallas_call(
        kernel,
        out_shape=(
            jax.ShapeDtypeStruct((ROWS, CH), BF16),
            jax.ShapeDtypeStruct((ROWS, CH), BF16),
            jax.ShapeDtypeStruct((8, 2 * CH), F32),
            jax.ShapeDtypeStruct((8, CH), F32),
            jax.ShapeDtypeStruct((TAPS, CH), F32),
            jax.ShapeDtypeStruct((8, 128), F32),
            jax.ShapeDtypeStruct((8, 128), F32),
        ),
        in_specs=[smem, hbm, hbm, vmem, vmem, vmem, hbm, hbm],
        out_specs=(hbm, hbm, vmem, vmem, vmem, vmem, vmem),
        scratch_shapes=[
            pltpu.VMEM((ROWS, CH), BF16),
            pltpu.VMEM((CH, 2 * CH), BF16),
            pltpu.VMEM((CH, CH), BF16),
            pltpu.VMEM((ROWS, CH), BF16),
            pltpu.VMEM((CB, 2, 8, 128), F32),
            pltpu.VMEM((CB, ROWS, 128), F32),
            pltpu.VMEM((CB, ROWS, 128), F32),
            pltpu.VMEM((CB, PROWS, 128), F32),
            pltpu.VMEM((CB, PROWS, 128), F32),
            pltpu.VMEM((CB, ROWS, 128), F32),
            pltpu.VMEM((CB, ROWS, 128), F32),
            pltpu.VMEM((CB, ROWS, 128), BF16),
            pltpu.VMEM((2 * CB, ROWS, 128), BF16),
            pltpu.VMEM((2, ROWS, CH), BF16),
            pltpu.VMEM((CB, 32, 8, 128), F32),
            pltpu.VMEM((8, 8, 128), F32),
            pltpu.VMEM((2, 8, 128), F32),
            pltpu.VMEM((2, 2, 8, 128), F32),
            pltpu.VMEM((2, 2, 8, 128), F32),
            pltpu.VMEM((2, NTM, 2, 8, 128), F32),
            pltpu.VMEM((2, NDP, 2, 8, 128), F32),
            pltpu.VMEM((16, 16, 128), BF16),
            pltpu.VMEM((32, 8, 128), F32),
            pltpu.VMEM((32, 8, 128), F32),
            pltpu.VMEM((32, 8, 128), F32),
            pltpu.VMEM((NTM, 2, 16, 128), BF16),
            pltpu.VMEM((2, 16, 128), BF16),
            pltpu.VMEM((NDP, 2, 16, 128), BF16),
            pltpu.VMEM((2, 16, 128), F32),
            pltpu.VMEM((NTM, 2, 16, 128), F32),
            *rs_scratch("a"),
            *rs_scratch("y"),
            *rs_scratch("dp"),
            dma((3,)),
            dma((4, 2)),
            dma((2,)),
            dma((4,)),
            dma((4,)),
            dma((2, NTM)),
            dma((2, NTM)),
            dma((2, NDP)),
            dma((2, NDP)),
            dma((NTM,)),
            dma((NTM,)),
            dma((NDP,)),
            dma((NDP,)),
            dma((NTM,)),
            dma((NTM,)),
            dma((NB, 19)),
            dma((NB, 19)),
        ],
        compiler_params=pltpu.CompilerParams(
            collective_id=0, has_side_effects=True, vmem_limit_bytes=62 << 20
        ),
        name="conformer_conv",
    )(
        lengths, frames[0], w_in, w_dw, bn_gain.reshape(8, 128), bn_bias.reshape(8, 128),
        w_out, cotangent[0],
    )
    out, gf, gwi, gwo, gk, gg, gb = pl.pallas_call(
        hand_over,
        out_shape=tuple(jax.ShapeDtypeStruct(o.shape, o.dtype) for o in outs),
        in_specs=[hbm] * 7,
        out_specs=(hbm,) * 7,
        scratch_shapes=[pltpu.VMEM(o.shape, o.dtype) for o in outs] + [dma((13, 2))],
        name="hand_over",
    )(*outs)
    return (out[None], gf[None], gwi, gwo, gk, gg.reshape(CH), gb.reshape(CH))


def solution(mesh):
    placed = (P("dp", "tm", None), P("dp"), P(), P(), P(), P(), P(), P("dp", "tm", None))
    return jax.shard_map(
        local,
        mesh=mesh,
        in_specs=placed,
        out_specs=(
            P("dp", "tm", None),
            P("dp", "tm", None),
            P(("dp", "tm"), None),
            P(("dp", "tm"), None),
            P(),
            P(),
            P(),
        ),
        check_vma=False,
    )
```
